512 devices in a mesh: shot: 4 (over x_lo, core), slab: 128 (over z, y, x_hi).
Axes of the slice: x: 4 (x_hi: 2, x_lo: 2; x = x_hi * 2 + x_lo), y: 4, z: 16, core: 2. Of those that a mesh axis runs over, the one named last changes fastest.
Arguments:
- lame_lambda: float32 [256, 32, 128], P('slab'), may hold values from 0.5 to 1.5
- lame_mu: float32 [256, 32, 128], P('slab'), may hold values from 0.3 to 0.8
- buoyancy: float32 [256, 32, 128], P('slab'), may hold values from 0.5 to 1
- forward_state: float32 [4, 9, 256, 32, 128], P('shot', None, 'slab'), may hold values from -6 to 6
- adjoint_state: float32 [4, 9, 256, 32, 128], P('shot', None, 'slab'), may hold values from -6 to 6
- source_wavelet: float32 [4, 8], P('shot'), may hold values from -20 to 20
- source_cell: int32 [4], P('shot'), may hold values from 0 to 1048575
- residual_traces: float32 [4, 8, 16384], P('shot', None, 'slab'), may hold values from -12 to 12
- receiver_slab: int32 [16384, 1], P('slab'), may hold values from 0 to 127; in each aligned block of 128 rows (0 to 127, 128 to 255, ...) at most 2 rows name the same one
- receiver_cell: int32 [16384], P('slab'), may hold values from 0 to 8191
Outputs:
- adjoint_start: float32 [4, 9, 256, 32, 128], P('shot', None, 'slab')
- lambda_gradient: float32 [256, 32, 128], P('slab', 'shot')
- mu_gradient: float32 [256, 32, 128], P('slab', 'shot')
The draws below stay inside these ranges and needn't reach their ends.
Inputs may be any that keep to these rules, and one draw needn't show every extreme that they name: `receiver_slab`: among the 128 receivers held by one index of slab, at most 2 lie in any one slab.
All inputs are finite; a program needn't handle non-finite values.
Results may differ from the reference program's by a relative error of at most 0.000067.
Values sent between devices are 32-bit elements; how exact they have to be, the bound alone decides.
No kernel may reach another device: no remote copies, remote signals or barrier semaphores. Data moves between devices by JAX's collectives and lax.ppermute only.
A program may use at most 64 MiB of HBM per device.

```python
import math
import jax
import jax.numpy as jnp
import numpy as np
from jax import lax

SX = 2
NY = 32
NZ = 128
REC_DEV = 128
STEPS = 8
SHOTS = 4
NX = 256
NREC = 16384
RCAP = 2
N_SLAB = 128


def plant(array, stream_key, smallest, high):
    index_at = [jax.random.randint(jax.random.fold_in(stream_key, axis), (), 0, length) for axis, length in enumerate(array.shape)]
    longest = array.shape.index(max(array.shape))
    neighbour = index_at[:longest] + [(index_at[longest] + 1) % array.shape[longest]] + index_at[longest + 1:]
    return array.at[tuple(index_at)].set(smallest).at[tuple(neighbour)].set(high)


def block_scale(rng, shape, shards, least, largest):
    def one(dim, parts):
        heights = jax.random.uniform(jax.random.fold_in(jax.random.fold_in(rng, 6), dim), (parts,), jnp.float32, least / len(shards), largest / len(shards))
        return jnp.repeat(jnp.exp(heights), shape[dim] // parts).reshape((-1,) + (1,) * (len(shape) - dim - 1))

    loudness = one(*shards[0])
    for cut in shards[1:]:
        loudness = loudness * one(*cut)
    return loudness


def assign_block(own_key, own, number, rows, number_of, top, bound, slope):
    order = jax.random.permutation(own_key, number_of)
    crowded, ordinary = load_shares(number_of, rows * top, bound, slope, True), load_shares(number_of, rows * top, bound, slope, False)
    places = jnp.arange(number_of)

    def named(lengths, rotation):
        used = int((lengths > 0).sum())
        fixed = max(1, used // 4)
        shifted = fixed + (places - fixed + rotation * (used - fixed)) % max(1, number_of - fixed)
        return jnp.zeros((number_of,), jnp.int32).at[order[jnp.where(places < fixed, places, shifted)]].set(jnp.asarray(lengths, jnp.int32))

    lengths = jnp.where(number % 4 == 0, named(crowded, number // 4), named(ordinary, number - number // 4 - 1))
    mixed = jax.random.permutation(jax.random.fold_in(own, 3), number_of)
    source_of, taker = mixed[0:number_of // 2 * 2:2], mixed[1:number_of // 2 * 2:2]
    margin = jnp.minimum(lengths[source_of] - 1, bound - lengths[taker]) // 2
    margin = jnp.where((source_of == order[0]) | (taker == order[0]) | (lengths[taker] == 0), 0, jnp.maximum(margin, 0))
    shifted = jax.random.randint(jax.random.fold_in(own, 4), (number_of // 2,), 0, 1 << 20) % (margin + 1)
    lengths = lengths.at[source_of].add(-shifted).at[taker].add(shifted)
    labels = jnp.searchsorted(jnp.cumsum(lengths), jnp.arange(rows * top), side="right").astype(jnp.int32)
    table = labels.reshape(top, rows).T
    table = table[jax.random.permutation(jax.random.fold_in(own, 1), rows)]
    rotation = jax.random.randint(jax.random.fold_in(own, 2), (rows, 1), 0, top)
    return jnp.take_along_axis(table, (jnp.arange(top)[None, :] + rotation) % top, axis=1)


def load_shares(amount, total, most, slope, full):
    portions = [(1 << 20) // math.isqrt(standing ** slope) + 1 for standing in range(1, amount + 1)]
    largest = most if full else min(most, max(-(-total // amount), total * portions[0] // sum(portions)))
    least = 1 if total - largest >= amount - 1 else 0
    counts, spare = [largest] + [least] * (amount - 1), total - largest - least * (amount - 1)
    while spare > 0:
        candidates = [i for i in range(1, amount) if counts[i] < largest] or [i for i in range(1, amount) if counts[i] < most]
        pool, budget = sum([portions[i] for i in candidates]), spare
        for i in candidates:
            extra = min(most - counts[i], max(1, budget * portions[i] // pool), spare)
            counts[i] = counts[i] + extra
            spare = spare - extra
    return np.array(counts)


def noise(rng, shape, width, limit, cuts=(), kind=jnp.bfloat16):
    drawn = jax.random.normal(rng, shape, jnp.float32) * width
    if len(cuts) > 0:
        drawn = block_scale(rng, shape, cuts, -0.22, 0.18) * drawn
    return jnp.clip(drawn, min=-limit, max=limit).astype(kind)


def setup_inputs(seed: int = 0) -> dict:
    key_of = jax.random.split(jax.random.key(seed), 11)
    lame_lambda = jnp.clip(jnp.exp(math.log(1.5) - 1.0986123 * jax.random.uniform(key_of[0], (NX, NY, NZ), jnp.float32) ** block_scale(key_of[0], (NX, NY, NZ), ((0, 128),), -0.2, 0.2)), 0.5, 1.5)
    lame_mu = jnp.clip(jnp.exp(math.log(0.8) - 0.98082923 * jax.random.uniform(key_of[1], (NX, NY, NZ), jnp.float32) ** block_scale(key_of[1], (NX, NY, NZ), ((0, 128),), -0.2, 0.2)), 0.3, 0.8)
    buoyancy = jnp.clip(jnp.exp(math.log(1.0) - 0.6931472 * jax.random.uniform(key_of[2], (NX, NY, NZ), jnp.float32) ** block_scale(key_of[2], (NX, NY, NZ), ((0, 128),), -0.2, 0.2)), 0.5, 1.0)
    forward_state = noise(key_of[3], (SHOTS, 9, NX, NY, NZ), 1.0, 6.0, ((0, 4), (2, 128)), jnp.float32)
    adjoint_state = noise(key_of[4], (SHOTS, 9, NX, NY, NZ), 1.0, 6.0, ((0, 4), (2, 128)), jnp.float32)
    source_wavelet = noise(key_of[5], (SHOTS, STEPS), 5.0, 20.0, ((0, 4),), jnp.float32)
    source_cell = plant(jax.random.randint(key_of[6], (SHOTS,), 0, NX * NY * NZ), jax.random.fold_in(key_of[6], 1), 0, (NX * NY * NZ) - 1).astype(jnp.int32)
    residual_traces = noise(key_of[7], (SHOTS, STEPS, NREC), 3.0, 12.0, ((0, 4), (2, 128)), jnp.float32)
    receiver_slab_keys = jax.random.split(jax.random.fold_in(key_of[8], 1), NREC // REC_DEV)
    receiver_slab_turns = jax.random.permutation(jax.random.fold_in(key_of[8], 3), NREC // REC_DEV)
    receiver_slab = jax.vmap(lambda own, number: assign_block(jax.random.fold_in(key_of[8], 2), own, number, REC_DEV, N_SLAB, 1, RCAP, 2))(receiver_slab_keys, receiver_slab_turns).reshape((NREC, 1))
    receiver_cell = plant(jax.random.randint(key_of[9], (NREC,), 0, SX * NY * NZ), jax.random.fold_in(key_of[9], 1), 0, (SX * NY * NZ) - 1).astype(jnp.int32)
    return dict(lame_lambda=lame_lambda, lame_mu=lame_mu, buoyancy=buoyancy, forward_state=forward_state, adjoint_state=adjoint_state, source_wavelet=source_wavelet, source_cell=source_cell, residual_traces=residual_traces, receiver_slab=receiver_slab, receiver_cell=receiver_cell)


TIME_STEP = 0.3


def next_cell(values, along):
    extent = values.shape[along]
    remainder = lax.slice_in_dim(values, 1, extent, axis=along)
    border = jnp.zeros_like(lax.slice_in_dim(values, 0, 1, axis=along))
    return jnp.concatenate([remainder, border], axis=along)


def prev_cell(values, along):
    extent = values.shape[along]
    remainder = lax.slice_in_dim(values, 0, extent - 1, axis=along)
    border = jnp.zeros_like(lax.slice_in_dim(values, 0, 1, axis=along))
    return jnp.concatenate([border, remainder], axis=along)


def velocity_update(velocity, stress, buoyancy, normal_after, shear_before):
    sigma_xx = stress[:, 0]
    sigma_yy = stress[:, 1]
    sigma_zz = stress[:, 2]
    sigma_xy = stress[:, 3]
    sigma_xz = stress[:, 4]
    sigma_yz = stress[:, 5]
    accel_x = (normal_after - sigma_xx) + (sigma_xy - prev_cell(sigma_xy, 2)) + (sigma_xz - prev_cell(sigma_xz, 3))
    accel_y = (sigma_xy - shear_before[:, 0]) + (next_cell(sigma_yy, 2) - sigma_yy) + (sigma_yz - prev_cell(sigma_yz, 3))
    accel_z = (sigma_xz - shear_before[:, 1]) + (sigma_yz - prev_cell(sigma_yz, 2)) + (next_cell(sigma_zz, 3) - sigma_zz)
    factor = TIME_STEP * buoyancy
    return jnp.stack([velocity[:, 0] - factor * accel_x, velocity[:, 1] - factor * accel_y, velocity[:, 2] - factor * accel_z], axis=1)


def stress_update(velocity, stress, lame_lambda, lame_mu, speed_before, speeds_after):
    speed_x = velocity[:, 0]
    speed_y = velocity[:, 1]
    speed_z = velocity[:, 2]
    strain_xx = speed_x - speed_before[:, 0]
    strain_yy = speed_y - prev_cell(speed_y, 2)
    strain_zz = speed_z - prev_cell(speed_z, 3)
    strain_xy = (next_cell(speed_x, 2) - speed_x) + (speeds_after[:, 0] - speed_y)
    strain_xz = (next_cell(speed_x, 3) - speed_x) + (speeds_after[:, 1] - speed_z)
    strain_yz = (next_cell(speed_y, 3) - speed_y) + (next_cell(speed_z, 2) - speed_z)
    dilation = strain_xx + strain_yy + strain_zz
    volume_term = lame_lambda * dilation
    twice_mu = 2.0 * lame_mu
    updated = jnp.stack([
        stress[:, 0] - TIME_STEP * (volume_term + twice_mu * strain_xx),
        stress[:, 1] - TIME_STEP * (volume_term + twice_mu * strain_yy),
        stress[:, 2] - TIME_STEP * (volume_term + twice_mu * strain_zz),
        stress[:, 3] - TIME_STEP * (lame_mu * strain_xy),
        stress[:, 4] - TIME_STEP * (lame_mu * strain_xz),
        stress[:, 5] - TIME_STEP * (lame_mu * strain_yz)], axis=1)
    return updated, (strain_xx, strain_yy, strain_zz, strain_xy, strain_xz, strain_yz)


def imaging(strains):
    strain_xx, strain_yy, strain_zz, strain_xy, strain_xz, strain_yz = strains
    dilation = strain_xx + strain_yy + strain_zz
    lambda_term = TIME_STEP * (dilation[0] * dilation[1])
    shear_term = 2.0 * (strain_xx[0] * strain_xx[1] + strain_yy[0] * strain_yy[1] + strain_zz[0] * strain_zz[1])
    shear_term = shear_term + strain_xy[0] * strain_xy[1] + strain_xz[0] * strain_xz[1] + strain_yz[0] * strain_yz[1]
    return lambda_term, TIME_STEP * shear_term


def reference(lame_lambda, lame_mu, buoyancy, forward_state, adjoint_state, source_wavelet, source_cell, residual_traces, receiver_slab, receiver_cell):
    extent_x, extent_y, extent_z = lame_lambda.shape
    total_cells = extent_x * extent_y * extent_z
    slab_cells = SX * NY * NZ
    targets = (receiver_slab[:, 0] * slab_cells + receiver_cell).astype(jnp.int32)
    grad_lambda = jnp.zeros(lame_lambda.shape, jnp.float32)
    grad_shear = jnp.zeros(lame_lambda.shape, jnp.float32)
    finals = []
    for shot_index in range(SHOTS):
        receiver_push = jnp.zeros((STEPS, total_cells), jnp.float32).at[:, targets].add(residual_traces[shot_index])
        receiver_push = receiver_push.reshape(STEPS, extent_x, extent_y, extent_z)
        source_spot = (jnp.arange(total_cells, dtype=jnp.int32) == source_cell[shot_index]).astype(jnp.float32).reshape(extent_x, extent_y, extent_z)
        wavefields = jnp.stack([forward_state[shot_index], adjoint_state[shot_index]])
        velocity = wavefields[:, 0:3]
        stress = wavefields[:, 3:9]
        for step_index in range(STEPS):
            velocity = velocity_update(velocity, stress, buoyancy, next_cell(stress[:, 0], 1), prev_cell(stress[:, 3:5], 2))
            stress, strains = stress_update(velocity, stress, lame_lambda, lame_mu, prev_cell(velocity[:, 0:1], 2), next_cell(velocity[:, 1:3], 2))
            lambda_term, shear_term = imaging(strains)
            grad_lambda = grad_lambda + lambda_term
            grad_shear = grad_shear + shear_term
            pushes = jnp.stack([source_spot * source_wavelet[shot_index, step_index], receiver_push[step_index]])
            stress = stress.at[:, 0:3].add(-TIME_STEP * pushes[:, None])
        finals.append(jnp.concatenate([velocity[1], stress[1]], axis=0))
    return jnp.stack(finals), grad_lambda, grad_shear
```

```python
import functools

import jax
import jax.numpy as jnp
from jax import lax
from jax.experimental import pallas as pl
from jax.experimental.pallas import tpu as pltpu
from jax.sharding import PartitionSpec as P

TIME_STEP = 0.3
CAP = 2
LANES = 128


def reach_steps(steps, planes, reach):
    counts = {}
    for e in range(-reach, reach + 1):
        gap = planes * (abs(e) - 1) + 1 if e else 0
        counts[e] = max(0, steps - gap)
    return counts


def message_lanes(counts):
    lanes, at = {}, 0
    for e in sorted(counts, key=abs):
        for slot in range(CAP):
            lanes[e, slot] = at
            at += 1 + counts[e]
    return lanes, at


def split3(x):
    hi = x.astype(jnp.bfloat16)
    rest = x - hi.astype(jnp.float32)
    mid = rest.astype(jnp.bfloat16)
    low = (rest - mid.astype(jnp.float32)).astype(jnp.bfloat16)
    return hi, mid, low


def dot_onehot(values, onehot, dims):
    hi, mid, low = split3(values)
    hot = onehot.astype(jnp.bfloat16)
    go = lambda part: lax.dot_general(part, hot, dims, preferred_element_type=jnp.float32)
    return go(hi) + (go(mid) + go(low))


def onehot_dot(onehot, values, dims):
    hi, mid, low = split3(values)
    hot = onehot.astype(jnp.bfloat16)
    go = lambda part: lax.dot_general(hot, part, dims, preferred_element_type=jnp.float32)
    return go(hi) + (go(mid) + go(low))


def letters_kernel(counts, lanes, reach, trace_ref, slab_ref, cell_ref, out_ref, rows_ref):
    steps, count = trace_ref.shape
    slab_col = jnp.broadcast_to(slab_ref[...], (count, count))
    slab_row = slab_col.astype(jnp.float32).T.astype(jnp.int32)
    sub = lax.broadcasted_iota(jnp.int32, (count, count), 0)
    lane = lax.broadcasted_iota(jnp.int32, (count, count), 1)
    same = jnp.where((slab_col == slab_row) & (lane < sub), 1.0, 0.0)
    slot_of = jnp.sum(same, axis=1, keepdims=True)
    table = jnp.concatenate(
        [trace_ref[...], cell_ref[...].astype(jnp.float32), jnp.zeros((16 - steps - 1, count), jnp.float32)], axis=0
    )
    src = lax.broadcasted_iota(jnp.int32, (16, LANES), 0)
    dst = lax.broadcasted_iota(jnp.int32, (16, LANES), 1)
    spread = jnp.zeros((16, LANES), jnp.float32)
    slot_lane = jnp.zeros((1, LANES), jnp.float32)
    one_lane = lax.broadcasted_iota(jnp.int32, (1, LANES), 1)
    for (e, slot), at in lanes.items():
        n = counts[e]
        spread = jnp.where((dst == at) & (src == steps), 1.0, spread)
        spread = jnp.where((dst > at) & (dst <= at + n) & (src == dst - at - 1), 1.0, spread)
        slot_lane = jnp.where((one_lane >= at) & (one_lane <= at + n), float(slot), slot_lane)
    wide = dot_onehot(table, spread, (((0,), (0,)), ((), ())))
    wide = jnp.where(slot_of == slot_lane, wide, 0.0)
    pick = jnp.where(slab_row == sub, 1.0, 0.0)
    rows = onehot_dot(pick, wide, (((1,), (0,)), ((), ())))
    rows_ref[...] = jnp.zeros_like(rows_ref)
    rows_ref[8 : 8 + count] = rows
    letter = jnp.zeros((count, LANES), jnp.float32)
    for e in range(-reach, reach + 1):
        start, end = lanes[e, 0], lanes[e, CAP - 1] + counts[e]
        letter = jnp.where((lane >= start) & (lane <= end), rows_ref[8 + e : 8 + e + count], letter)
    out_ref[...] = letter


def window_kernel(
    counts, lanes, reach, steps, meta_ref, wavelet_ref, *refs
):
    blocks = refs[: 2 * reach]
    own_f, own_a, lam_in, mu_in, buo_in, letters_ref, end_ref, grad_ref, state, par, push = refs[2 * reach :]
    planes, rows, depth = lam_in.shape
    halo = planes * reach
    for i, block in enumerate(blocks):
        e = i - reach if i < reach else i - reach + 1
        at = halo + planes * e
        for f in range(2):
            for c in range(9):
                state[f, c, at : at + planes] = block[9 * f + c]
        for c in range(3):
            par[c, at : at + planes] = block[18 + c]
    for c in range(9):
        state[0, c, halo : halo + planes] = own_f[c]
        state[1, c, halo : halo + planes] = own_a[c]
    for c, ref in enumerate((lam_in, mu_in, buo_in)):
        par[c, halo : halo + planes] = ref[...]
    letters = letters_ref[...]
    letters_t = letters.T
    sources = letters.shape[0]
    lane_iota = lax.broadcasted_iota(jnp.int32, (sources, depth), 1)
    row_iota = lax.broadcasted_iota(jnp.int32, (planes * rows, sources), 0)
    for e in range(-reach, reach + 1):
        n = counts[e]
        lefts, rights = [], []
        for slot in range(CAP):
            at = lanes[e, slot]
            cell_col = letters[:, at : at + 1].astype(jnp.int32)
            rights.append(jnp.where(lane_iota == (cell_col & (depth - 1)), 1.0, 0.0))
            cell_row = letters_t[at : at + 1, :].astype(jnp.int32) // depth
            hit = row_iota == cell_row
            lefts.append(
                jnp.concatenate([jnp.where(hit, letters_t[at + 1 + k : at + 2 + k, :], 0.0) for k in range(n)], axis=0)
            )
        left = jnp.concatenate(lefts, axis=1)
        right = jnp.concatenate(rights, axis=0)
        sums = TIME_STEP * dot_onehot(left, right, (((1,), (0,)), ((), ())))
        for k in range(n):
            push[k, halo + planes * e : halo + planes * (e + 1)] = sums[
                k * planes * rows : (k + 1) * planes * rows
            ].reshape(planes, rows, depth)

    y_iota = lax.broadcasted_iota(jnp.int32, (rows, depth), 0)
    z_iota = lax.broadcasted_iota(jnp.int32, (rows, depth), 1)
    y_first, y_last = y_iota == 0, y_iota == rows - 1
    z_first, z_last = z_iota == 0, z_iota == depth - 1

    def prev_y(x):
        return jnp.where(y_first, 0.0, pltpu.roll(x, 1, 0))

    def next_y(x):
        return jnp.where(y_last, 0.0, pltpu.roll(x, rows - 1, 0))

    def prev_z(x):
        return jnp.where(z_first, 0.0, pltpu.roll(x, 1, 1))

    def next_z(x):
        return jnp.where(z_last, 0.0, pltpu.roll(x, depth - 1, 1))

    def velocity(p, along_x, across):
        factor = TIME_STEP * par[2, p]
        for f in range(2):
            sxy, sxz = state[f, 6, p], state[f, 7, p]
            if along_x:
                accel = (state[f, 3, p + 1] - state[f, 3, p]) + (sxy - prev_y(sxy)) + (sxz - prev_z(sxz))
                state[f, 0, p] = state[f, 0, p] - factor * accel
            if across:
                syy, szz, syz = state[f, 4, p], state[f, 5, p], state[f, 8, p]
                accel = (sxy - state[f, 6, p - 1]) + (next_y(syy) - syy) + (syz - prev_z(syz))
                state[f, 1, p] = state[f, 1, p] - factor * accel
                accel = (sxz - state[f, 7, p - 1]) + (syz - prev_y(syz)) + (next_z(szz) - szz)
                state[f, 2, p] = state[f, 2, p] - factor * accel

    def stress(p, k, image):
        lam = TIME_STEP * par[0, p]
        mu = TIME_STEP * par[1, p]
        twice = 2.0 * mu
        strains = []
        for f in range(2):
            vx, vy, vz = state[f, 0, p], state[f, 1, p], state[f, 2, p]
            exx = vx - state[f, 0, p - 1]
            eyy = vy - prev_y(vy)
            ezz = vz - prev_z(vz)
            exy = (next_y(vx) - vx) + (state[f, 1, p + 1] - vy)
            exz = (next_z(vx) - vx) + (state[f, 2, p + 1] - vz)
            eyz = (next_z(vy) - vy) + (next_y(vz) - vz)
            tr = exx + eyy + ezz
            volume = lam * tr
            if f == 1:
                volume = volume + push[k, p]
            state[f, 3, p] = state[f, 3, p] - (volume + twice * exx)
            state[f, 4, p] = state[f, 4, p] - (volume + twice * eyy)
            state[f, 5, p] = state[f, 5, p] - (volume + twice * ezz)
            state[f, 6, p] = state[f, 6, p] - mu * exy
            state[f, 7, p] = state[f, 7, p] - mu * exz
            state[f, 8, p] = state[f, 8, p] - mu * eyz
            strains.append((exx, eyy, ezz, exy, exz, eyz, tr))
        if image:
            (axx, ayy, azz, axy, axz, ayz, atr), (bxx, byy, bzz, bxy, bxz, byz, btr) = strains
            return atr * btr, 2.0 * (axx * bxx + ayy * byy + azz * bzz) + axy * bxy + axz * bxz + ayz * byz
        return None

    cell = meta_ref[0]
    src_plane = cell // (rows * depth) - planes * meta_ref[1] + halo
    src_at = cell % (rows * depth)
    spot = jnp.where(y_iota * depth + z_iota == src_at, TIME_STEP, 0.0)

    totals = [[jnp.zeros((rows, depth), jnp.float32)] * 2 for _ in range(planes)]
    for k in range(steps):
        m = steps - 1 - k
        low, high = halo - m, halo + planes + m
        velocity(low - 1, True, False)

        @pl.loop(low, high)
        def _(p):
            velocity(p, True, True)

        velocity(high, False, True)
        if m:
            @pl.loop(low, halo)
            def _(p):
                stress(p, k, False)

            @pl.loop(halo + planes, high)
            def _(p):
                stress(p, k, False)

        for p in range(planes):
            first, second = stress(halo + p, k, True)
            totals[p] = [totals[p][0] + first, totals[p][1] + second]

        @pl.when((src_plane >= low) & (src_plane < high))
        def _():
            shot = wavelet_ref[k] * spot
            for c in (3, 4, 5):
                state[0, c, src_plane] = state[0, c, src_plane] - shot

    for c in range(9):
        end_ref[c] = state[1, c, halo : halo + planes]
    share = rows // grad_ref.shape[0]
    for p in range(planes):
        for g in range(2):
            total = TIME_STEP * totals[p][g]
            for j in range(grad_ref.shape[0]):
                grad_ref[j, g, p] = total[j * share : (j + 1) * share]


def vmem():
    return pl.BlockSpec(memory_space=pltpu.VMEM)


def smem():
    return pl.BlockSpec(memory_space=pltpu.SMEM)


def shards(
    lame_lambda,
    lame_mu,
    buoyancy,
    forward_state,
    adjoint_state,
    source_wavelet,
    source_cell,
    residual_traces,
    receiver_slab,
    receiver_cell,
):
    planes, rows, depth = lame_lambda.shape
    steps = source_wavelet.shape[1]
    slabs = lax.axis_size("slab")
    shots = lax.axis_size("shot")
    reach = -(-steps // planes)
    counts = reach_steps(steps, planes, reach)
    lanes, _ = message_lanes(counts)
    my_slab = lax.axis_index("slab")

    letters = pl.pallas_call(
        functools.partial(letters_kernel, counts, lanes, reach),
        out_shape=jax.ShapeDtypeStruct((slabs, LANES), jnp.float32),
        in_specs=[vmem()] * 3,
        out_specs=vmem(),
        scratch_shapes=[pltpu.VMEM((slabs + 16, LANES), jnp.float32)],
        name="letters",
    )(residual_traces[0], receiver_slab, receiver_cell[None, :])

    block = jnp.concatenate(
        [forward_state[0], adjoint_state[0], lame_lambda[None], lame_mu[None], buoyancy[None]], axis=0
    )
    offsets = [e for e in range(-reach, reach + 1) if e]
    near = {}
    for e in offsets:
        near[e] = lax.ppermute(
            block, "slab", [(i + e, i) for i in range(slabs) if 0 <= i + e < slabs]
        )
    got = lax.all_to_all(letters, "slab", 0, 0, tiled=True)

    extent = planes + 2 * planes * reach
    meta = jnp.concatenate([source_cell, my_slab[None].astype(jnp.int32)])
    end, grads = pl.pallas_call(
        functools.partial(window_kernel, counts, lanes, reach, steps),
        out_shape=(
            jax.ShapeDtypeStruct((9, planes, rows, depth), jnp.float32),
            jax.ShapeDtypeStruct((shots, 2, planes, rows // shots, depth), jnp.float32),
        ),
        in_specs=[smem(), smem()] + [vmem()] * (2 * reach + 6),
        out_specs=(vmem(), vmem()),
        scratch_shapes=[
            pltpu.VMEM((2, 9, extent, rows, depth), jnp.float32),
            pltpu.VMEM((3, extent, rows, depth), jnp.float32),
            pltpu.VMEM((steps, extent, rows, depth), jnp.float32),
        ],
        compiler_params=pltpu.CompilerParams(vmem_limit_bytes=48 * 1024 * 1024),
        name="window",
    )(
        meta,
        source_wavelet[0],
        *[near[e] for e in offsets],
        forward_state[0],
        adjoint_state[0],
        lame_lambda,
        lame_mu,
        buoyancy,
        got,
    )
    parts = lax.all_to_all(grads, "shot", 0, 0, tiled=True)
    total = jnp.sum(parts, axis=0)
    return (end[None], total[0], total[1])


def solution(mesh):
    in_specs = (
        P("slab", None, None),
        P("slab", None, None),
        P("slab", None, None),
        P("shot", None, "slab", None, None),
        P("shot", None, "slab", None, None),
        P("shot", None),
        P("shot"),
        P("shot", None, "slab"),
        P("slab", None),
        P("slab"),
    )
    out_specs = (
        P("shot", None, "slab", None, None),
        P("slab", "shot", None),
        P("slab", "shot", None),
    )
    return jax.shard_map(shards, mesh=mesh, in_specs=in_specs, out_specs=out_specs, check_vma=False)
```

```python
import functools

import jax
import jax.numpy as jnp
from jax import lax
from jax.experimental import pallas as pl
from jax.experimental.pallas import tpu as pltpu
from jax.sharding import PartitionSpec as P

TIME_STEP = 0.3
CAP = 2
LANES = 128
FIELDS = 21
NOTES = 16


def reach_steps(steps, planes, reach):
    counts = {}
    for e in range(-reach, reach + 1):
        gap = planes * (abs(e) - 1) + 1 if e else 0
        counts[e] = max(0, steps - gap)
    return counts


def message_lanes(counts):
    lanes, at = {}, 0
    for e in sorted(counts, key=abs):
        for slot in range(CAP):
            lanes[e, slot] = at
            at += 1 + counts[e]
    return lanes, at


def split3(x):
    hi = x.astype(jnp.bfloat16)
    rest = x - hi.astype(jnp.float32)
    mid = rest.astype(jnp.bfloat16)
    low = (rest - mid.astype(jnp.float32)).astype(jnp.bfloat16)
    return hi, mid, low


def dot_onehot(values, onehot, dims):
    hi, mid, low = split3(values)
    hot = onehot.astype(jnp.bfloat16)
    go = lambda part: lax.dot_general(part, hot, dims, preferred_element_type=jnp.float32)
    return go(hi) + (go(mid) + go(low))


def onehot_dot(onehot, values, dims):
    hi, mid, low = split3(values)
    hot = onehot.astype(jnp.bfloat16)
    go = lambda part: lax.dot_general(hot, part, dims, preferred_element_type=jnp.float32)
    return go(hi) + (go(mid) + go(low))


def letters_kernel(counts, lanes, reach, steps, note_ref, out_ref, rows_ref):
    count = note_ref.shape[1]
    notes = note_ref[...]
    slab_row = jnp.broadcast_to(notes[steps : steps + 1], (count, count))
    slab_col = slab_row.T
    sub = lax.broadcasted_iota(jnp.int32, (count, count), 0)
    lane = lax.broadcasted_iota(jnp.int32, (count, count), 1)
    same = jnp.where((slab_col == slab_row) & (lane < sub), 1.0, 0.0)
    slot_of = jnp.sum(same, axis=1, keepdims=True)
    src = lax.broadcasted_iota(jnp.int32, (NOTES, LANES), 0)
    dst = lax.broadcasted_iota(jnp.int32, (NOTES, LANES), 1)
    spread = jnp.zeros((NOTES, LANES), jnp.float32)
    slot_lane = jnp.zeros((1, LANES), jnp.float32)
    one_lane = lax.broadcasted_iota(jnp.int32, (1, LANES), 1)
    for (e, slot), at in lanes.items():
        n = counts[e]
        spread = jnp.where((dst == at) & (src == steps + 1), 1.0, spread)
        spread = jnp.where((dst > at) & (dst <= at + n) & (src == dst - at - 1), 1.0, spread)
        slot_lane = jnp.where((one_lane >= at) & (one_lane <= at + n), float(slot), slot_lane)
    wide = dot_onehot(notes, spread, (((0,), (0,)), ((), ())))
    wide = jnp.where(slot_of == slot_lane, wide, 0.0)
    pick = jnp.where(slab_row == sub.astype(jnp.float32), 1.0, 0.0)
    rows = onehot_dot(pick, wide, (((1,), (0,)), ((), ())))
    rows_ref[...] = jnp.zeros_like(rows_ref)
    rows_ref[8 : 8 + count] = rows
    letter = jnp.zeros((count, LANES), jnp.float32)
    for e in range(-reach, reach + 1):
        start, end = lanes[e, 0], lanes[e, CAP - 1] + counts[e]
        letter = jnp.where((lane >= start) & (lane <= end), rows_ref[8 + e : 8 + e + count], letter)
    out_ref[...] = letter


def pack_kernel(cell_ref, f_ref, a_ref, lam_ref, mu_ref, buo_ref, trace_ref, slab_ref, spot_ref, wave_ref, out_ref):
    planes, rows, depth = lam_ref.shape
    one = planes * rows
    for f, ref in enumerate((f_ref, a_ref)):
        for c in range(9):
            at = (9 * f + c) * one
            out_ref[at : at + one] = ref[c].reshape(one, depth)
    for c, ref in enumerate((lam_ref, mu_ref, buo_ref)):
        at = (18 + c) * one
        out_ref[at : at + one] = ref[...].reshape(one, depth)
    at, steps = FIELDS * one, trace_ref.shape[0]
    out_ref[at + 8 : at + NOTES] = jnp.zeros((NOTES - 8, depth), jnp.float32)
    out_ref[at : at + steps] = trace_ref[...]
    out_ref[at + steps : at + steps + 1] = slab_ref[...].astype(jnp.float32)
    out_ref[at + steps + 1 : at + steps + 2] = spot_ref[...].astype(jnp.float32)
    out_ref[at + steps + 2 : at + steps + 3, 0:steps] = wave_ref[...]
    out_ref[at + steps + 3 : at + steps + 4] = jnp.full((1, depth), cell_ref[0], jnp.int32).astype(jnp.float32)


def window_kernel(
    counts, lanes, reach, steps, planes, rows, meta_ref, *refs
):
    mine = refs[: reach + 1]
    theirs = refs[reach + 1 : 2 * reach + 1]
    letters_ref, end_ref, grad_ref, state, push, sems = refs[2 * reach + 1 :]
    depth = state.shape[2]
    one = planes * rows
    core, slab = meta_ref[0], meta_ref[1]
    copies = []
    for o in range(reach + 1):
        at = reach + core + (2 * core - 1) * o
        copies.append(pltpu.make_async_copy(mine[o], state.at[at], sems.at[o]))
    for o in range(reach):
        at = reach + 1 - core + (1 - 2 * core) * o
        copies.append(pltpu.make_async_copy(theirs[o], state.at[at], sems.at[reach + 1 + o]))
    for copy in copies:
        copy.start()
    halo = planes * (reach + core)
    letters = letters_ref[...]
    letters_t = letters.T
    sources = letters.shape[0]
    lane_iota = lax.broadcasted_iota(jnp.int32, (sources, depth), 1)
    row_iota = lax.broadcasted_iota(jnp.int32, (one, sources), 0)
    for e in range(-reach, reach + 1):
        n = counts[e]
        lefts, rights = [], []
        for slot in range(CAP):
            at = lanes[e, slot]
            cell_col = letters[:, at : at + 1].astype(jnp.int32)
            rights.append(jnp.where(lane_iota == (cell_col & (depth - 1)), 1.0, 0.0))
            cell_row = letters_t[at : at + 1, :].astype(jnp.int32) // depth
            hit = row_iota == cell_row
            lefts.append(
                jnp.concatenate([jnp.where(hit, letters_t[at + 1 + k : at + 2 + k, :], 0.0) for k in range(n)], axis=0)
            )
        left = jnp.concatenate(lefts, axis=1)
        right = jnp.concatenate(rights, axis=0)
        sums = TIME_STEP * dot_onehot(left, right, (((1,), (0,)), ((), ())))
        for k in range(n):
            push[k, pl.ds(halo + planes * e, planes)] = sums[k * one : (k + 1) * one].reshape(planes, rows, depth)
    for copy in copies:
        copy.wait()

    y_iota = lax.broadcasted_iota(jnp.int32, (rows, depth), 0)
    z_iota = lax.broadcasted_iota(jnp.int32, (rows, depth), 1)
    y_first, y_last = y_iota == 0, y_iota == rows - 1
    z_first, z_last = z_iota == 0, z_iota == depth - 1

    def prev_y(x):
        return jnp.where(y_first, 0.0, pltpu.roll(x, 1, 0))

    def next_y(x):
        return jnp.where(y_last, 0.0, pltpu.roll(x, rows - 1, 0))

    def prev_z(x):
        return jnp.where(z_first, 0.0, pltpu.roll(x, 1, 1))

    def next_z(x):
        return jnp.where(z_last, 0.0, pltpu.roll(x, depth - 1, 1))

    class Plane:
        def __init__(self, p):
            self.block = p // planes
            self.row = (p % planes) * rows

        def where(self, f, c):
            return self.block, pl.ds(pl.multiple_of(self.row + (9 * f + c) * one, rows), rows)

        def get(self, f, c):
            return state[self.where(f, c)]

        def put(self, f, c, value):
            state[self.where(f, c)] = value

    def velocity(p, along_x, across):
        here, after, before = Plane(p), Plane(p + 1), Plane(p - 1)
        factor = TIME_STEP * here.get(2, 2)
        for f in range(2):
            sxy, sxz = here.get(f, 6), here.get(f, 7)
            if along_x:
                accel = (after.get(f, 3) - here.get(f, 3)) + (sxy - prev_y(sxy)) + (sxz - prev_z(sxz))
                here.put(f, 0, here.get(f, 0) - factor * accel)
            if across:
                syy, szz, syz = here.get(f, 4), here.get(f, 5), here.get(f, 8)
                accel = (sxy - before.get(f, 6)) + (next_y(syy) - syy) + (syz - prev_z(syz))
                here.put(f, 1, here.get(f, 1) - factor * accel)
                accel = (sxz - before.get(f, 7)) + (syz - prev_y(syz)) + (next_z(szz) - szz)
                here.put(f, 2, here.get(f, 2) - factor * accel)

    def stress(p, k, image):
        here, after, before = Plane(p), Plane(p + 1), Plane(p - 1)
        lam = TIME_STEP * here.get(2, 0)
        mu = TIME_STEP * here.get(2, 1)
        twice = 2.0 * mu
        strains = []
        for f in range(2):
            vx, vy, vz = here.get(f, 0), here.get(f, 1), here.get(f, 2)
            exx = vx - before.get(f, 0)
            eyy = vy - prev_y(vy)
            ezz = vz - prev_z(vz)
            exy = (next_y(vx) - vx) + (after.get(f, 1) - vy)
            exz = (next_z(vx) - vx) + (after.get(f, 2) - vz)
            eyz = (next_z(vy) - vy) + (next_y(vz) - vz)
            tr = exx + eyy + ezz
            volume = lam * tr
            if f == 1:
                volume = volume + push[k, p]
            here.put(f, 3, here.get(f, 3) - (volume + twice * exx))
            here.put(f, 4, here.get(f, 4) - (volume + twice * eyy))
            here.put(f, 5, here.get(f, 5) - (volume + twice * ezz))
            here.put(f, 6, here.get(f, 6) - mu * exy)
            here.put(f, 7, here.get(f, 7) - mu * exz)
            here.put(f, 8, here.get(f, 8) - mu * eyz)
            strains.append((exx, eyy, ezz, exy, exz, eyz, tr))
        if image:
            (axx, ayy, azz, axy, axz, ayz, atr), (bxx, byy, bzz, bxy, bxz, byz, btr) = strains
            return atr * btr, 2.0 * (axx * bxx + ayy * byy + azz * bzz) + axy * bxy + axz * bxz + ayz * byz
        return None

    notes = state[reach + core, FIELDS * one + steps : FIELDS * one + steps + 8]
    wave, cell = notes[2:3], jnp.max(notes[3:4]).astype(jnp.int32)
    src_plane = cell // (rows * depth) - planes * slab + halo
    src_at = cell % (rows * depth)
    spot = jnp.where(y_iota * depth + z_iota == src_at, TIME_STEP, 0.0)

    totals = [[jnp.zeros((rows, depth), jnp.float32)] * 2 for _ in range(planes)]
    for k in range(steps):
        m = steps - 1 - k
        low, high = halo - m, halo + planes + m
        velocity(low - 1, True, False)

        @pl.loop(low, high)
        def _(p):
            velocity(p, True, True)

        velocity(high, False, True)
        if m:
            @pl.loop(low, halo)
            def _(p):
                stress(p, k, False)

            @pl.loop(halo + planes, high)
            def _(p):
                stress(p, k, False)

        for p in range(planes):
            first, second = stress(halo + p, k, True)
            totals[p] = [totals[p][0] + first, totals[p][1] + second]

        @pl.when((src_plane >= low) & (src_plane < high))
        def _():
            shot = wave[:, k : k + 1] * spot
            there = Plane(src_plane)
            for c in (3, 4, 5):
                there.put(0, c, there.get(0, c) - shot)

    for c in range(9):
        at = (9 + c) * one
        end_ref[c] = state[reach + core, at : at + one].reshape(planes, rows, depth)
    shots = grad_ref.shape[0] // 2
    share = rows // shots
    for p in range(planes):
        for g in range(2):
            total = TIME_STEP * totals[p][g]
            for j in range(shots):
                for h in range(2):
                    grad_ref[2 * j + h, g, p] = jnp.where(core == h, total[j * share : (j + 1) * share], 0.0)


def vmem():
    return pl.BlockSpec(memory_space=pltpu.VMEM)


def smem():
    return pl.BlockSpec(memory_space=pltpu.SMEM)


def anywhere():
    return pl.BlockSpec(memory_space=pl.ANY)


def shards(
    lame_lambda,
    lame_mu,
    buoyancy,
    forward_state,
    adjoint_state,
    source_wavelet,
    source_cell,
    residual_traces,
    receiver_slab,
    receiver_cell,
):
    planes, rows, depth = lame_lambda.shape
    steps = source_wavelet.shape[1]
    slabs = lax.axis_size("slab")
    shots = lax.axis_size("shot")
    axes = ("shot", "slab")
    reach = -(-steps // planes)
    counts = reach_steps(steps, planes, reach)
    lanes, _ = message_lanes(counts)
    height = FIELDS * planes * rows + NOTES

    def at(s, d):
        return ((s & ~1) | (d & 1)) * slabs + ((d & ~1) | (s & 1))

    every = [(s, d) for s in range(shots) for d in range(slabs)]
    swap = [(s * slabs + d, at(s, d)) for s, d in every]
    across = [(at(s, d), at(s, d ^ 1)) for s, d in every]
    team = [[at(s, d) for d in range(slabs)] for s in range(shots)]
    pair = [[s * slabs + 2 * q + h for s in range(shots) for h in range(2)] for q in range(slabs // 2)]

    block = pl.pallas_call(
        pack_kernel,
        out_shape=jax.ShapeDtypeStruct((height, depth), jnp.float32),
        in_specs=[smem()] + [vmem()] * 9,
        out_specs=vmem(),
        name="pack",
    )(
        source_cell,
        forward_state[0],
        adjoint_state[0],
        lame_lambda,
        lame_mu,
        buoyancy,
        residual_traces[0],
        receiver_slab.reshape(1, -1),
        receiver_cell.reshape(1, -1),
        source_wavelet,
    )
    mine = [lax.ppermute(block, axes, swap)]
    for o in range(1, reach + 1):
        pairs = []
        for s, d in every:
            i = d + o if d % 2 else d - o
            if 0 <= i < slabs:
                pairs.append((s * slabs + i, at(s, d)))
        mine.append(lax.ppermute(block, axes, pairs))

    letters = pl.pallas_call(
        functools.partial(letters_kernel, counts, lanes, reach, steps),
        grid=(1,),
        out_shape=jax.ShapeDtypeStruct((slabs, LANES), jnp.float32),
        in_specs=[pl.BlockSpec((NOTES, depth), lambda i: (FIELDS * planes * rows // NOTES, 0))],
        out_specs=pl.BlockSpec((slabs, LANES), lambda i: (0, 0)),
        scratch_shapes=[pltpu.VMEM((slabs + 16, LANES), jnp.float32)],
        name="letters",
    )(mine[0])
    got = lax.all_to_all(letters, axes, 0, 0, axis_index_groups=team, tiled=True)
    *mine, got = lax.optimization_barrier((*mine, got))
    theirs = [lax.ppermute(mine[o], axes, across) for o in range(reach)]

    my_shot, my_slab = lax.axis_index("shot"), lax.axis_index("slab")
    core = my_shot & 1
    meta = jnp.stack([core, (my_slab & ~1) | core]).astype(jnp.int32)
    extent = planes * (2 * reach + 2)
    end, grads = pl.pallas_call(
        functools.partial(window_kernel, counts, lanes, reach, steps, planes, rows),
        out_shape=(
            jax.ShapeDtypeStruct((9, planes, rows, depth), jnp.float32),
            jax.ShapeDtypeStruct((2 * shots, 2, planes, rows // shots, depth), jnp.float32),
        ),
        in_specs=[smem()] + [anywhere()] * (2 * reach + 1) + [vmem()],
        out_specs=(vmem(), vmem()),
        scratch_shapes=[
            pltpu.VMEM((2 * reach + 2, height, depth), jnp.float32),
            pltpu.VMEM((steps, extent, rows, depth), jnp.float32),
            pltpu.SemaphoreType.DMA((2 * reach + 1,)),
        ],
        compiler_params=pltpu.CompilerParams(vmem_limit_bytes=40 * 1024 * 1024),
        name="window",
    )(meta, *mine, *theirs, got)
    end = lax.ppermute(end, axes, swap)
    parts = lax.all_to_all(grads, axes, 0, 0, axis_index_groups=pair, tiled=True)
    total = jnp.sum(parts, axis=0)
    return (end[None], total[0], total[1])


def solution(mesh):
    in_specs = (
        P("slab", None, None),
        P("slab", None, None),
        P("slab", None, None),
        P("shot", None, "slab", None, None),
        P("shot", None, "slab", None, None),
        P("shot", None),
        P("shot"),
        P("shot", None, "slab"),
        P("slab", None),
        P("slab"),
    )
    out_specs = (
        P("shot", None, "slab", None, None),
        P("slab", "shot", None),
        P("slab", "shot", None),
    )
    return jax.shard_map(shards, mesh=mesh, in_specs=in_specs, out_specs=out_specs, check_vma=False)
```

```python
import functools

import jax
import jax.numpy as jnp
from jax import lax
from jax.experimental import pallas as pl
from jax.experimental.pallas import tpu as pltpu
from jax.sharding import PartitionSpec as P

TIME_STEP = 0.3
CAP = 2
LANES = 128
FIELDS = 21
NOTES = 16


def reach_steps(steps, planes, reach):
    counts = {}
    for e in range(-reach, reach + 1):
        gap = planes * (abs(e) - 1) + 1 if e else 0
        counts[e] = max(0, steps - gap)
    return counts


def message_lanes(counts):
    lanes, at = {}, 0
    for e in sorted(counts, key=abs):
        for slot in range(CAP):
            lanes[e, slot] = at
            at += 1 + counts[e]
    return lanes, at


def split3(x):
    hi = x.astype(jnp.bfloat16)
    rest = x - hi.astype(jnp.float32)
    mid = rest.astype(jnp.bfloat16)
    low = (rest - mid.astype(jnp.float32)).astype(jnp.bfloat16)
    return hi, mid, low


def dot_onehot(values, onehot, dims):
    hi, mid, low = split3(values)
    hot = onehot.astype(jnp.bfloat16)
    go = lambda part: lax.dot_general(part, hot, dims, preferred_element_type=jnp.float32)
    return go(hi) + (go(mid) + go(low))


def onehot_dot(onehot, values, dims):
    hi, mid, low = split3(values)
    hot = onehot.astype(jnp.bfloat16)
    go = lambda part: lax.dot_general(hot, part, dims, preferred_element_type=jnp.float32)
    return go(hi) + (go(mid) + go(low))


def letters_kernel(counts, lanes, reach, steps, note_ref, out_ref, rows_ref):
    count = note_ref.shape[1]
    notes = note_ref[...]
    slab_row = jnp.broadcast_to(notes[steps : steps + 1], (count, count))
    slab_col = slab_row.T
    sub = lax.broadcasted_iota(jnp.int32, (count, count), 0)
    lane = lax.broadcasted_iota(jnp.int32, (count, count), 1)
    same = jnp.where((slab_col == slab_row) & (lane < sub), 1.0, 0.0)
    slot_of = jnp.sum(same, axis=1, keepdims=True)
    src = lax.broadcasted_iota(jnp.int32, (NOTES, LANES), 0)
    dst = lax.broadcasted_iota(jnp.int32, (NOTES, LANES), 1)
    spread = jnp.zeros((NOTES, LANES), jnp.float32)
    slot_lane = jnp.zeros((1, LANES), jnp.float32)
    one_lane = lax.broadcasted_iota(jnp.int32, (1, LANES), 1)
    for (e, slot), at in lanes.items():
        n = counts[e]
        spread = jnp.where((dst == at) & (src == steps + 1), 1.0, spread)
        spread = jnp.where((dst > at) & (dst <= at + n) & (src == dst - at - 1), 1.0, spread)
        slot_lane = jnp.where((one_lane >= at) & (one_lane <= at + n), float(slot), slot_lane)
    wide = dot_onehot(notes, spread, (((0,), (0,)), ((), ())))
    wide = jnp.where(slot_of == slot_lane, wide, 0.0)
    pick = jnp.where(slab_row == sub.astype(jnp.float32), 1.0, 0.0)
    rows = onehot_dot(pick, wide, (((1,), (0,)), ((), ())))
    rows_ref[...] = jnp.zeros_like(rows_ref)
    rows_ref[8 : 8 + count] = rows
    letter = jnp.zeros((count, LANES), jnp.float32)
    for e in range(-reach, reach + 1):
        start, end = lanes[e, 0], lanes[e, CAP - 1] + counts[e]
        letter = jnp.where((lane >= start) & (lane <= end), rows_ref[8 + e : 8 + e + count], letter)
    out_ref[...] = letter


def pack_kernel(cell_ref, f_ref, a_ref, lam_ref, mu_ref, buo_ref, trace_ref, slab_ref, spot_ref, wave_ref, out_ref):
    planes, rows, depth = lam_ref.shape
    one = planes * rows
    for c in range(9):
        out_ref[c * one : (c + 1) * one] = f_ref[c].reshape(one, depth)
        at = 12 * one + NOTES + c * one
        out_ref[at : at + one] = a_ref[c].reshape(one, depth)
    for c, ref in enumerate((lam_ref, mu_ref, buo_ref)):
        out_ref[(9 + c) * one : (10 + c) * one] = TIME_STEP * ref[...].reshape(one, depth)
    at, steps = 12 * one, trace_ref.shape[0]
    out_ref[at + 8 : at + NOTES] = jnp.zeros((NOTES - 8, depth), jnp.float32)
    out_ref[at : at + steps] = trace_ref[...]
    out_ref[at + steps : at + steps + 1] = slab_ref[...].astype(jnp.float32)
    out_ref[at + steps + 1 : at + steps + 2] = spot_ref[...].astype(jnp.float32)
    out_ref[at + steps + 2 : at + steps + 3, 0:steps] = wave_ref[...]
    out_ref[at + steps + 3 : at + steps + 4] = jnp.full((1, depth), cell_ref[0], jnp.int32).astype(jnp.float32)


class Window:
    def __init__(self, state, planes, rows, field, params, slab):
        self.state, self.planes, self.rows = state, planes, rows
        self.first = planes * slab
        self.one = planes * rows
        self.height = 12 * self.one + NOTES
        self.field, self.params = field, params
        self.own = pl.multiple_of(slab * self.height, 16)
        depth = state.shape[1]
        self.y = lax.broadcasted_iota(jnp.int32, (rows, depth), 0)
        self.z = lax.broadcasted_iota(jnp.int32, (rows, depth), 1)
        self.ends = (self.y == 0, self.y == rows - 1, self.z == 0, self.z == depth - 1)

    def fill(self, mine, theirs, sems, core, reach, start):
        copies = []
        for o in range(reach + 1):
            copies.append((mine[o], reach + core + (2 * core - 1) * o))
        for o in range(reach):
            copies.append((theirs[o], reach + 1 - core + (1 - 2 * core) * o))
        copies = [
            pltpu.make_async_copy(
                block.at[pl.ds(start, self.height)],
                self.state.at[pl.ds(pl.multiple_of(at * self.height, 16), self.height)],
                sems.at[i],
            )
            for i, (block, at) in enumerate(copies)
        ]
        for copy in copies:
            copy.start()
        return copies

    def base(self, p):
        return (p // self.planes) * self.height + (p % self.planes) * self.rows

    def at(self, base, row):
        return pl.ds(pl.multiple_of(self.own + (base + row), 8), self.rows)

    def get(self, base, c):
        return self.state[self.at(base, self.field + c * self.one)]

    def param(self, base, c):
        return self.state[self.at(base, self.params + c * self.one)]

    def put(self, base, values):
        for c, value in values:
            self.state[self.at(base, self.field + c * self.one)] = value

    def prev_y(self, x):
        return jnp.where(self.ends[0], 0.0, pltpu.roll(x, 1, 0))

    def next_y(self, x):
        return jnp.where(self.ends[1], 0.0, pltpu.roll(x, x.shape[0] - 1, 0))

    def prev_z(self, x):
        return jnp.where(self.ends[2], 0.0, pltpu.roll(x, 1, 1))

    def next_z(self, x):
        return jnp.where(self.ends[3], 0.0, pltpu.roll(x, x.shape[1] - 1, 1))

    def velocity(self, p, along_x=True, across=True):
        here, after, before = self.base(p), self.base(p + 1), self.base(p - 1)
        get = self.get
        factor = self.param(here, 2)
        sxy, sxz = get(here, 6), get(here, 7)
        out = []
        if along_x:
            accel = (get(after, 3) - get(here, 3)) + (sxy - self.prev_y(sxy)) + (sxz - self.prev_z(sxz))
            out.append((0, get(here, 0) - factor * accel))
        if across:
            syy, szz, syz = get(here, 4), get(here, 5), get(here, 8)
            accel = (sxy - get(before, 6)) + (self.next_y(syy) - syy) + (syz - self.prev_z(syz))
            out.append((1, get(here, 1) - factor * accel))
            accel = (sxz - get(before, 7)) + (syz - self.prev_y(syz)) + (self.next_z(szz) - szz)
            out.append((2, get(here, 2) - factor * accel))
        return here, out

    def stress(self, p, push=None):
        here, after, before = self.base(p), self.base(p + 1), self.base(p - 1)
        get = self.get
        lam, mu = self.param(here, 0), self.param(here, 1)
        twice = 2.0 * mu
        vx, vy, vz = get(here, 0), get(here, 1), get(here, 2)
        exx = vx - get(before, 0)
        eyy = vy - self.prev_y(vy)
        ezz = vz - self.prev_z(vz)
        exy = (self.next_y(vx) - vx) + (get(after, 1) - vy)
        exz = (self.next_z(vx) - vx) + (get(after, 2) - vz)
        eyz = (self.next_z(vy) - vy) + (self.next_y(vz) - vz)
        volume = lam * (exx + eyy + ezz)
        if push is not None:
            volume = volume + push
        out = [
            (3, get(here, 3) - (volume + twice * exx)),
            (4, get(here, 4) - (volume + twice * eyy)),
            (5, get(here, 5) - (volume + twice * ezz)),
            (6, get(here, 6) - mu * exy),
            (7, get(here, 7) - mu * exz),
            (8, get(here, 8) - mu * eyz),
        ]
        return here, out, (exx, eyy, ezz, exy, exz, eyz)

    def step(self, k, steps, push, see):
        m = steps - 1 - k
        low, high = -m, self.planes + m
        pushed = lambda p: None if push is None else push[k, self.first + p]
        ready = []
        for p in range(low - 1, high + 1):
            ready.append(self.velocity(p, along_x=p < high, across=p >= low))
            if p >= low:
                self.put(*ready.pop(0))
        self.put(*ready.pop(0))
        for p in range(low, high):
            here, out, strains = self.stress(p, pushed(p))
            self.put(here, out)
            if 0 <= p < self.planes:
                see(k, p, strains)


def forward_kernel(reach, steps, planes, rows, meta_ref, *refs):
    mine, theirs = refs[: reach + 1], refs[reach + 1 : 2 * reach + 1]
    strain_ref, state, sems = refs[2 * reach + 1 :]
    depth = state.shape[1]
    one = planes * rows
    core, slab = meta_ref[0], meta_ref[1]
    window = Window(state, planes, rows, 0, 9 * one, reach + core)
    for copy in window.fill(mine, theirs, sems, core, reach, 0):
        copy.wait()
    halo = planes * (reach + core)
    at = pl.multiple_of((reach + core) * window.height + 12 * one + steps, 8)
    notes = state[pl.ds(at, 8)]
    wave, cell = notes[2:3], jnp.max(notes[3:4]).astype(jnp.int32)
    src_plane = cell // (rows * depth) - planes * slab
    spot = jnp.where(window.y * depth + window.z == cell % (rows * depth), TIME_STEP, 0.0)

    def see(k, p, strains):
        for c, strain in enumerate(strains):
            strain_ref[k, c, p] = strain

    for k in range(steps):
        window.step(k, steps, None, see)
        m = steps - 1 - k

        @pl.when((src_plane >= -m) & (src_plane < planes + m))
        def _():
            shot = wave[:, k : k + 1] * spot
            there = window.base(src_plane + planes * reach) - reach * window.height
            window.put(there, [(c, window.get(there, c) - shot) for c in (3, 4, 5)])


def adjoint_kernel(counts, lanes, reach, steps, planes, rows, meta_ref, *refs):
    mine, theirs = refs[: reach + 1], refs[reach + 1 : 2 * reach + 1]
    letters_ref, strain_ref, end_ref, grad_ref, state, push, sems = refs[2 * reach + 1 :]
    depth = state.shape[1]
    one = planes * rows
    core = meta_ref[0]
    window = Window(state, planes, rows, 3 * one + NOTES, 0, reach + core)
    copies = window.fill(mine, theirs, sems, core, reach, 9 * one)
    halo = planes * (reach + core)
    letters = letters_ref[...]
    letters_t = letters.T
    sources = letters.shape[0]
    lane_iota = lax.broadcasted_iota(jnp.int32, (sources, depth), 1)
    row_iota = lax.broadcasted_iota(jnp.int32, (one, sources), 0)
    for e in range(-reach, reach + 1):
        n = counts[e]
        lefts, rights = [], []
        for slot in range(CAP):
            at = lanes[e, slot]
            cell_col = letters[:, at : at + 1].astype(jnp.int32)
            rights.append(jnp.where(lane_iota == (cell_col & (depth - 1)), 1.0, 0.0))
            cell_row = letters_t[at : at + 1, :].astype(jnp.int32) // depth
            hit = row_iota == cell_row
            lefts.append(
                jnp.concatenate([jnp.where(hit, letters_t[at + 1 + k : at + 2 + k, :], 0.0) for k in range(n)], axis=0)
            )
        left = jnp.concatenate(lefts, axis=1)
        right = jnp.concatenate(rights, axis=0)
        sums = TIME_STEP * dot_onehot(left, right, (((1,), (0,)), ((), ())))
        for k in range(n):
            push[k, pl.ds(halo + planes * e, planes)] = sums[k * one : (k + 1) * one].reshape(planes, rows, depth)
    for copy in copies:
        copy.wait()

    totals = [[jnp.zeros((rows, depth), jnp.float32)] * 2 for _ in range(planes)]

    def see(k, p, strains):
        axx, ayy, azz, axy, axz, ayz = (strain_ref[k, c, p] for c in range(6))
        bxx, byy, bzz, bxy, bxz, byz = strains
        first = (axx + ayy + azz) * (bxx + byy + bzz)
        second = 2.0 * (axx * bxx + ayy * byy + azz * bzz) + axy * bxy + axz * bxz + ayz * byz
        totals[p] = [totals[p][0] + first, totals[p][1] + second]

    for k in range(steps):
        window.step(k, steps, push, see)

    own = pl.multiple_of((reach + core) * window.height + window.field, 16)
    final = pltpu.make_async_copy(state.at[pl.ds(own, 9 * one)], end_ref, sems.at[2 * reach + 1])
    final.start()
    shots = grad_ref.shape[0] // 2
    share = rows // shots
    for p in range(planes):
        for g in range(2):
            total = TIME_STEP * totals[p][g]
            for j in range(shots):
                for h in range(2):
                    grad_ref[2 * j + h, g, p] = jnp.where(core == h, total[j * share : (j + 1) * share], 0.0)
    final.wait()


def vmem():
    return pl.BlockSpec(memory_space=pltpu.VMEM)


def smem():
    return pl.BlockSpec(memory_space=pltpu.SMEM)


def hbm():
    return pl.BlockSpec(memory_space=pltpu.HBM)


def shards(
    lame_lambda,
    lame_mu,
    buoyancy,
    forward_state,
    adjoint_state,
    source_wavelet,
    source_cell,
    residual_traces,
    receiver_slab,
    receiver_cell,
):
    planes, rows, depth = lame_lambda.shape
    one = planes * rows
    steps = source_wavelet.shape[1]
    slabs = lax.axis_size("slab")
    shots = lax.axis_size("shot")
    axes = ("shot", "slab")
    reach = -(-steps // planes)
    counts = reach_steps(steps, planes, reach)
    lanes, _ = message_lanes(counts)
    height = FIELDS * one + NOTES

    def at(s, d):
        return ((s & ~1) | (d & 1)) * slabs + ((d & ~1) | (s & 1))

    every = [(s, d) for s in range(shots) for d in range(slabs)]
    swap = [(s * slabs + d, at(s, d)) for s, d in every]
    across = [(at(s, d), at(s, d ^ 1)) for s, d in every]
    team = [[at(s, d) for d in range(slabs)] for s in range(shots)]
    pair = [[s * slabs + 2 * q + h for s in range(shots) for h in range(2)] for q in range(slabs // 2)]

    block = pl.pallas_call(
        pack_kernel,
        out_shape=jax.ShapeDtypeStruct((height, depth), jnp.float32),
        in_specs=[smem()] + [vmem()] * 9,
        out_specs=vmem(),
        name="pack",
    )(
        source_cell,
        forward_state[0],
        adjoint_state[0],
        lame_lambda,
        lame_mu,
        buoyancy,
        residual_traces[0],
        receiver_slab.reshape(1, -1),
        receiver_cell.reshape(1, -1),
        source_wavelet,
    )
    mine = [lax.ppermute(block, axes, swap)]
    for o in range(1, reach + 1):
        pairs = []
        for s, d in every:
            i = d + o if d % 2 else d - o
            if 0 <= i < slabs:
                pairs.append((s * slabs + i, at(s, d)))
        mine.append(lax.ppermute(block, axes, pairs))

    letters = pl.pallas_call(
        functools.partial(letters_kernel, counts, lanes, reach, steps),
        grid=(1,),
        out_shape=jax.ShapeDtypeStruct((slabs, LANES), jnp.float32),
        in_specs=[pl.BlockSpec((NOTES, depth), lambda i: (12 * one // NOTES, 0))],
        out_specs=pl.BlockSpec((slabs, LANES), lambda i: (0, 0)),
        scratch_shapes=[pltpu.VMEM((slabs + 16, LANES), jnp.float32)],
        name="letters",
    )(mine[0])
    got = lax.all_to_all(letters, axes, 0, 0, axis_index_groups=team, tiled=True)
    my_shot, my_slab = lax.axis_index("shot"), lax.axis_index("slab")
    core = my_shot & 1
    meta = jnp.stack([core, (my_slab & ~1) | core]).astype(jnp.int32)
    extent = planes * (2 * reach + 2)
    held = pltpu.VMEM(((2 * reach + 2) * (12 * one + NOTES), depth), jnp.float32)
    cost = pl.CostEstimate(flops=60_000_000, transcendentals=0, bytes_accessed=16_000_000)

    def share_and_run(mine):
        theirs = [lax.ppermute(mine[o], axes, across) for o in range(reach)]
        strains = pl.pallas_call(
            functools.partial(forward_kernel, reach, steps, planes, rows),
            out_shape=jax.ShapeDtypeStruct((steps, 6, planes, rows, depth), jnp.float32),
            in_specs=[smem()] + [hbm()] * (2 * reach + 1),
            out_specs=vmem(),
            scratch_shapes=[held, pltpu.SemaphoreType.DMA((2 * reach + 1,))],
            compiler_params=pltpu.CompilerParams(vmem_limit_bytes=60 * 1024 * 1024),
            cost_estimate=cost,
            name="forward",
        )(meta, *mine, *theirs)
        return (*theirs, strains)

    def nothing(mine):
        return (*mine[:reach], jnp.zeros((steps, 6, planes, rows, depth), jnp.float32))

    *theirs, strains = lax.cond(my_slab < slabs, share_and_run, nothing, mine)
    end, grads = pl.pallas_call(
        functools.partial(adjoint_kernel, counts, lanes, reach, steps, planes, rows),
        out_shape=(
            jax.ShapeDtypeStruct((9 * one, depth), jnp.float32),
            jax.ShapeDtypeStruct((2 * shots, 2, planes, rows // shots, depth), jnp.float32),
        ),
        in_specs=[smem()] + [hbm()] * (2 * reach + 1) + [vmem()] * 2,
        out_specs=(hbm(), vmem()),
        scratch_shapes=[
            held,
            pltpu.VMEM((steps, extent, rows, depth), jnp.float32),
            pltpu.SemaphoreType.DMA((2 * reach + 2,)),
        ],
        compiler_params=pltpu.CompilerParams(vmem_limit_bytes=60 * 1024 * 1024),
        cost_estimate=cost,
        name="adjoint",
    )(meta, *mine, *theirs, got, strains)
    end = lax.ppermute(end, axes, swap)
    parts = lax.all_to_all(grads, axes, 0, 0, axis_index_groups=pair, tiled=True)
    total = jnp.sum(parts, axis=0)
    return (end.reshape(1, 9, planes, rows, depth), total[0], total[1])


def solution(mesh):
    in_specs = (
        P("slab", None, None),
        P("slab", None, None),
        P("slab", None, None),
        P("shot", None, "slab", None, None),
        P("shot", None, "slab", None, None),
        P("shot", None),
        P("shot"),
        P("shot", None, "slab"),
        P("slab", None),
        P("slab"),
    )
    out_specs = (
        P("shot", None, "slab", None, None),
        P("slab", "shot", None),
        P("slab", "shot", None),
    )
    return jax.shard_map(shards, mesh=mesh, in_specs=in_specs, out_specs=out_specs, check_vma=False)
```

```python
import functools

import jax
import jax.numpy as jnp
from jax import lax
from jax.experimental import pallas as pl
from jax.experimental.pallas import tpu as pltpu
from jax.sharding import PartitionSpec as P

TIME_STEP = 0.3
CAP = 2
LANES = 128
FIELDS = 21
NOTES = 16


def reach_steps(steps, planes, reach):
    counts = {}
    for e in range(-reach, reach + 1):
        gap = planes * (abs(e) - 1) + 1 if e else 0
        counts[e] = max(0, steps - gap)
    return counts


def message_lanes(counts):
    lanes, at = {}, 0
    for e in sorted(counts, key=abs):
        for slot in range(CAP):
            lanes[e, slot] = at
            at += 1 + counts[e]
    return lanes, at


def split3(x):
    hi = x.astype(jnp.bfloat16)
    rest = x - hi.astype(jnp.float32)
    mid = rest.astype(jnp.bfloat16)
    low = (rest - mid.astype(jnp.float32)).astype(jnp.bfloat16)
    return hi, mid, low


def dot_onehot(values, onehot, dims):
    hi, mid, low = split3(values)
    hot = onehot.astype(jnp.bfloat16)
    go = lambda part: lax.dot_general(part, hot, dims, preferred_element_type=jnp.float32)
    return go(hi) + (go(mid) + go(low))


def onehot_dot(onehot, values, dims):
    hi, mid, low = split3(values)
    hot = onehot.astype(jnp.bfloat16)
    go = lambda part: lax.dot_general(hot, part, dims, preferred_element_type=jnp.float32)
    return go(hi) + (go(mid) + go(low))


def letters_kernel(counts, lanes, reach, steps, note_ref, out_ref, rows_ref):
    count = note_ref.shape[1]
    notes = note_ref[...]
    slab_row = jnp.broadcast_to(notes[steps : steps + 1], (count, count))
    slab_col = slab_row.T
    sub = lax.broadcasted_iota(jnp.int32, (count, count), 0)
    lane = lax.broadcasted_iota(jnp.int32, (count, count), 1)
    same = jnp.where((slab_col == slab_row) & (lane < sub), 1.0, 0.0)
    slot_of = jnp.sum(same, axis=1, keepdims=True)
    src = lax.broadcasted_iota(jnp.int32, (NOTES, LANES), 0)
    dst = lax.broadcasted_iota(jnp.int32, (NOTES, LANES), 1)
    spread = jnp.zeros((NOTES, LANES), jnp.float32)
    slot_lane = jnp.zeros((1, LANES), jnp.float32)
    one_lane = lax.broadcasted_iota(jnp.int32, (1, LANES), 1)
    for (e, slot), at in lanes.items():
        n = counts[e]
        spread = jnp.where((dst == at) & (src == steps + 1), 1.0, spread)
        spread = jnp.where((dst > at) & (dst <= at + n) & (src == dst - at - 1), 1.0, spread)
        slot_lane = jnp.where((one_lane >= at) & (one_lane <= at + n), float(slot), slot_lane)
    wide = dot_onehot(notes, spread, (((0,), (0,)), ((), ())))
    wide = jnp.where(slot_of == slot_lane, wide, 0.0)
    pick = jnp.where(slab_row == sub.astype(jnp.float32), 1.0, 0.0)
    rows = onehot_dot(pick, wide, (((1,), (0,)), ((), ())))
    rows_ref[...] = jnp.zeros_like(rows_ref)
    rows_ref[8 : 8 + count] = rows
    letter = jnp.zeros((count, LANES), jnp.float32)
    for e in range(-reach, reach + 1):
        start, end = lanes[e, 0], lanes[e, CAP - 1] + counts[e]
        letter = jnp.where((lane >= start) & (lane <= end), rows_ref[8 + e : 8 + e + count], letter)
    out_ref[...] = letter


def pack_kernel(cell_ref, f_ref, a_ref, lam_ref, mu_ref, buo_ref, trace_ref, slab_ref, spot_ref, wave_ref, out_ref):
    planes, rows, depth = lam_ref.shape
    one = planes * rows
    for c in range(9):
        out_ref[c * one : (c + 1) * one] = f_ref[c].reshape(one, depth)
        at = 12 * one + NOTES + c * one
        out_ref[at : at + one] = a_ref[c].reshape(one, depth)
    for c, ref in enumerate((lam_ref, mu_ref, buo_ref)):
        out_ref[(9 + c) * one : (10 + c) * one] = TIME_STEP * ref[...].reshape(one, depth)
    at, steps = 12 * one, trace_ref.shape[0]
    out_ref[at + 8 : at + NOTES] = jnp.zeros((NOTES - 8, depth), jnp.float32)
    out_ref[at : at + steps] = trace_ref[...]
    out_ref[at + steps : at + steps + 1] = slab_ref[...].astype(jnp.float32)
    out_ref[at + steps + 1 : at + steps + 2] = spot_ref[...].astype(jnp.float32)
    out_ref[at + steps + 2 : at + steps + 3, 0:steps] = wave_ref[...]
    out_ref[at + steps + 3 : at + steps + 4] = jnp.full((1, depth), cell_ref[0], jnp.int32).astype(jnp.float32)


class Window:
    def __init__(self, state, planes, rows, field, params, slab):
        self.state, self.planes, self.rows = state, planes, rows
        self.first = planes * slab
        self.one = planes * rows
        self.height = 12 * self.one + NOTES
        self.field, self.params = field, params
        self.own = pl.multiple_of(slab * self.height, 16)
        depth = state.shape[1]
        self.y = lax.broadcasted_iota(jnp.int32, (rows, depth), 0)
        self.z = lax.broadcasted_iota(jnp.int32, (rows, depth), 1)
        self.ends = (self.y == 0, self.y == rows - 1, self.z == 0, self.z == depth - 1)

    def fill(self, mine, theirs, sems, core, reach, start):
        copies = []
        for o in range(reach + 1):
            copies.append((mine[o], reach + core + (2 * core - 1) * o))
        for o in range(reach):
            copies.append((theirs[o], reach + 1 - core + (1 - 2 * core) * o))
        copies = [
            pltpu.make_async_copy(
                block.at[pl.ds(start, self.height)],
                self.state.at[pl.ds(pl.multiple_of(at * self.height, 16), self.height)],
                sems.at[i],
            )
            for i, (block, at) in enumerate(copies)
        ]
        for copy in copies:
            copy.start()
        return copies

    def base(self, p):
        return (p // self.planes) * self.height + (p % self.planes) * self.rows

    def at(self, base, row):
        return pl.ds(pl.multiple_of(self.own + (base + row), 8), self.rows)

    def get(self, base, c):
        return self.state[self.at(base, self.field + c * self.one)]

    def param(self, base, c):
        return self.state[self.at(base, self.params + c * self.one)]

    def put(self, base, values):
        for c, value in values:
            self.state[self.at(base, self.field + c * self.one)] = value

    def prev_y(self, x):
        return jnp.where(self.ends[0], 0.0, pltpu.roll(x, 1, 0))

    def next_y(self, x):
        return jnp.where(self.ends[1], 0.0, pltpu.roll(x, x.shape[0] - 1, 0))

    def prev_z(self, x):
        return jnp.where(self.ends[2], 0.0, pltpu.roll(x, 1, 1))

    def next_z(self, x):
        return jnp.where(self.ends[3], 0.0, pltpu.roll(x, x.shape[1] - 1, 1))

    def velocity(self, p, along_x=True, across=True):
        here, after, before = self.base(p), self.base(p + 1), self.base(p - 1)
        get = self.get
        factor = self.param(here, 2)
        sxy, sxz = get(here, 6), get(here, 7)
        out = []
        if along_x:
            accel = (get(after, 3) - get(here, 3)) + (sxy - self.prev_y(sxy)) + (sxz - self.prev_z(sxz))
            out.append((0, get(here, 0) - factor * accel))
        if across:
            syy, szz, syz = get(here, 4), get(here, 5), get(here, 8)
            accel = (sxy - get(before, 6)) + (self.next_y(syy) - syy) + (syz - self.prev_z(syz))
            out.append((1, get(here, 1) - factor * accel))
            accel = (sxz - get(before, 7)) + (syz - self.prev_y(syz)) + (self.next_z(szz) - szz)
            out.append((2, get(here, 2) - factor * accel))
        return here, out

    def stress(self, p, push=None):
        here, after, before = self.base(p), self.base(p + 1), self.base(p - 1)
        get = self.get
        lam, mu = self.param(here, 0), self.param(here, 1)
        twice = 2.0 * mu
        vx, vy, vz = get(here, 0), get(here, 1), get(here, 2)
        exx = vx - get(before, 0)
        eyy = vy - self.prev_y(vy)
        ezz = vz - self.prev_z(vz)
        exy = (self.next_y(vx) - vx) + (get(after, 1) - vy)
        exz = (self.next_z(vx) - vx) + (get(after, 2) - vz)
        eyz = (self.next_z(vy) - vy) + (self.next_y(vz) - vz)
        volume = lam * (exx + eyy + ezz)
        if push is not None:
            volume = volume + push
        out = [
            (3, get(here, 3) - (volume + twice * exx)),
            (4, get(here, 4) - (volume + twice * eyy)),
            (5, get(here, 5) - (volume + twice * ezz)),
            (6, get(here, 6) - mu * exy),
            (7, get(here, 7) - mu * exz),
            (8, get(here, 8) - mu * eyz),
        ]
        return here, out, (exx, eyy, ezz, exy, exz, eyz)

    def step(self, k, steps, push, see):
        m = steps - 1 - k
        low, high = -m, self.planes + m
        pushed = lambda p: None if push is None else push[k, self.first + p]
        ready = []
        for p in range(low - 1, high + 1):
            ready.append(self.velocity(p, along_x=p < high, across=p >= low))
            if p >= low:
                self.put(*ready.pop(0))
        self.put(*ready.pop(0))
        for p in range(low, high):
            here, out, strains = self.stress(p, pushed(p))
            self.put(here, out)
            if 0 <= p < self.planes:
                see(k, p, strains)


def forward_kernel(reach, steps, planes, rows, meta_ref, *refs):
    mine, theirs = refs[: reach + 1], refs[reach + 1 : 2 * reach + 1]
    strain_ref, state, sems = refs[2 * reach + 1 :]
    depth = state.shape[1]
    one = planes * rows
    core, slab = meta_ref[0], meta_ref[1]
    window = Window(state, planes, rows, 0, 9 * one, reach + core)
    for copy in window.fill(mine, theirs, sems, core, reach, 0):
        copy.wait()
    halo = planes * (reach + core)
    at = pl.multiple_of((reach + core) * window.height + 12 * one + steps, 8)
    notes = state[pl.ds(at, 8)]
    wave, cell = notes[2:3], jnp.max(notes[3:4]).astype(jnp.int32)
    src_plane = cell // (rows * depth) - planes * slab
    spot = jnp.where(window.y * depth + window.z == cell % (rows * depth), TIME_STEP, 0.0)

    def see(k, p, strains):
        for c, strain in enumerate(strains):
            strain_ref[k, c, p] = strain

    for k in range(steps):
        window.step(k, steps, None, see)
        m = steps - 1 - k

        @pl.when((src_plane >= -m) & (src_plane < planes + m))
        def _():
            shot = wave[:, k : k + 1] * spot
            there = window.base(src_plane + planes * reach) - reach * window.height
            window.put(there, [(c, window.get(there, c) - shot) for c in (3, 4, 5)])


def adjoint_kernel(counts, lanes, reach, steps, planes, rows, meta_ref, *refs):
    mine, theirs = refs[: reach + 1], refs[reach + 1 : 2 * reach + 1]
    letters_ref, strain_ref, end_ref, grad_ref, state, push, sems = refs[2 * reach + 1 :]
    depth = state.shape[1]
    one = planes * rows
    core = meta_ref[0]
    window = Window(state, planes, rows, 3 * one + NOTES, 0, reach + core)
    copies = window.fill(mine, theirs, sems, core, reach, 9 * one)
    halo = planes * (reach + core)
    letters = letters_ref[...]
    letters_t = letters.T
    sources = letters.shape[0]
    lane_iota = lax.broadcasted_iota(jnp.int32, (sources, depth), 1)
    row_iota = lax.broadcasted_iota(jnp.int32, (one, sources), 0)
    for e in range(-reach, reach + 1):
        n = counts[e]
        lefts, rights = [], []
        for slot in range(CAP):
            at = lanes[e, slot]
            cell_col = letters[:, at : at + 1].astype(jnp.int32)
            rights.append(jnp.where(lane_iota == (cell_col & (depth - 1)), 1.0, 0.0))
            cell_row = letters_t[at : at + 1, :].astype(jnp.int32) // depth
            hit = row_iota == cell_row
            lefts.append(
                jnp.concatenate([jnp.where(hit, letters_t[at + 1 + k : at + 2 + k, :], 0.0) for k in range(n)], axis=0)
            )
        left = jnp.concatenate(lefts, axis=1)
        right = jnp.concatenate(rights, axis=0)
        sums = TIME_STEP * dot_onehot(left, right, (((1,), (0,)), ((), ())))
        for k in range(n):
            push[k, pl.ds(halo + planes * e, planes)] = sums[k * one : (k + 1) * one].reshape(planes, rows, depth)
    for copy in copies:
        copy.wait()

    totals = [[jnp.zeros((rows, depth), jnp.float32)] * 2 for _ in range(planes)]

    def see(k, p, strains):
        axx, ayy, azz, axy, axz, ayz = (strain_ref[k, c, p] for c in range(6))
        bxx, byy, bzz, bxy, bxz, byz = strains
        first = (axx + ayy + azz) * (bxx + byy + bzz)
        second = 2.0 * (axx * bxx + ayy * byy + azz * bzz) + axy * bxy + axz * bxz + ayz * byz
        totals[p] = [totals[p][0] + first, totals[p][1] + second]

    for k in range(steps):
        window.step(k, steps, push, see)

    own = pl.multiple_of((reach + core) * window.height + window.field, 16)
    final = pltpu.make_async_copy(state.at[pl.ds(own, 9 * one)], end_ref, sems.at[2 * reach + 1])
    final.start()
    shots = grad_ref.shape[0] // 2
    share = rows // shots
    for p in range(planes):
        for g in range(2):
            total = TIME_STEP * totals[p][g]
            for j in range(shots):
                for h in range(2):
                    grad_ref[2 * j + h, g, p] = jnp.where(core == h, total[j * share : (j + 1) * share], 0.0)
    final.wait()


def vmem():
    return pl.BlockSpec(memory_space=pltpu.VMEM)


def smem():
    return pl.BlockSpec(memory_space=pltpu.SMEM)


def hbm():
    return pl.BlockSpec(memory_space=pltpu.HBM)


def shards(
    lame_lambda,
    lame_mu,
    buoyancy,
    forward_state,
    adjoint_state,
    source_wavelet,
    source_cell,
    residual_traces,
    receiver_slab,
    receiver_cell,
):
    planes, rows, depth = lame_lambda.shape
    one = planes * rows
    steps = source_wavelet.shape[1]
    slabs = lax.axis_size("slab")
    shots = lax.axis_size("shot")
    axes = ("shot", "slab")
    reach = -(-steps // planes)
    counts = reach_steps(steps, planes, reach)
    lanes, _ = message_lanes(counts)
    height = FIELDS * one + NOTES

    def at(s, d):
        return ((s & ~1) | (d & 1)) * slabs + ((d & ~1) | (s & 1))

    every = [(s, d) for s in range(shots) for d in range(slabs)]
    swap = [(s * slabs + d, at(s, d)) for s, d in every]
    across = [(at(s, d), at(s, d ^ 1)) for s, d in every]
    team = [[at(s, d) for d in range(slabs)] for s in range(shots)]
    pair = [[s * slabs + 2 * q + h for s in range(shots) for h in range(2)] for q in range(slabs // 2)]

    block = pl.pallas_call(
        pack_kernel,
        out_shape=jax.ShapeDtypeStruct((height, depth), jnp.float32),
        in_specs=[smem()] + [vmem()] * 9,
        out_specs=vmem(),
        name="pack",
    )(
        source_cell,
        forward_state[0],
        adjoint_state[0],
        lame_lambda,
        lame_mu,
        buoyancy,
        residual_traces[0],
        receiver_slab.reshape(1, -1),
        receiver_cell.reshape(1, -1),
        source_wavelet,
    )
    mine = [lax.ppermute(block, axes, swap)]
    for o in range(1, reach + 1):
        pairs = []
        for s, d in every:
            i = d + o if d % 2 else d - o
            if 0 <= i < slabs:
                pairs.append((s * slabs + i, at(s, d)))
        mine.append(lax.ppermute(block, axes, pairs))

    letters = pl.pallas_call(
        functools.partial(letters_kernel, counts, lanes, reach, steps),
        grid=(1,),
        out_shape=jax.ShapeDtypeStruct((slabs, LANES), jnp.float32),
        in_specs=[pl.BlockSpec((NOTES, depth), lambda i: (12 * one // NOTES, 0))],
        out_specs=pl.BlockSpec((slabs, LANES), lambda i: (0, 0)),
        scratch_shapes=[pltpu.VMEM((slabs + 16, LANES), jnp.float32)],
        name="letters",
    )(mine[0])
    got = lax.all_to_all(letters, axes, 0, 0, axis_index_groups=team, tiled=True)
    my_shot, my_slab = lax.axis_index("shot"), lax.axis_index("slab")
    core = my_shot & 1
    meta = jnp.stack([core, (my_slab & ~1) | core]).astype(jnp.int32)
    extent = planes * (2 * reach + 2)
    held = pltpu.VMEM(((2 * reach + 2) * (12 * one + NOTES), depth), jnp.float32)
    cost = pl.CostEstimate(flops=60_000_000, transcendentals=0, bytes_accessed=16_000_000)

    def share(blocks):
        return [lax.ppermute(block, axes, across) for block in blocks]

    here = my_slab < slabs
    theirs = []
    theirs += lax.cond(here, share, lambda blocks: blocks, mine[0:2])
    theirs += lax.cond(here, share, lambda blocks: blocks, mine[2:3])
    theirs += lax.cond(here, share, lambda blocks: blocks, mine[3:reach])

    def run(blocks):
        strains = pl.pallas_call(
            functools.partial(forward_kernel, reach, steps, planes, rows),
            out_shape=jax.ShapeDtypeStruct((steps, 6, planes, rows, depth), jnp.float32),
            in_specs=[smem()] + [hbm()] * (2 * reach + 1),
            out_specs=vmem(),
            scratch_shapes=[held, pltpu.SemaphoreType.DMA((2 * reach + 1,))],
            compiler_params=pltpu.CompilerParams(vmem_limit_bytes=60 * 1024 * 1024),
            cost_estimate=cost,
            name="forward",
        )(meta, *blocks)
        return strains

    strains = lax.cond(here, run, lambda blocks: jnp.zeros((steps, 6, planes, rows, depth), jnp.float32), (*mine, *theirs))
    end, grads = pl.pallas_call(
        functools.partial(adjoint_kernel, counts, lanes, reach, steps, planes, rows),
        out_shape=(
            jax.ShapeDtypeStruct((9 * one, depth), jnp.float32),
            jax.ShapeDtypeStruct((2 * shots, 2, planes, rows // shots, depth), jnp.float32),
        ),
        in_specs=[smem()] + [hbm()] * (2 * reach + 1) + [vmem()] * 2,
        out_specs=(hbm(), vmem()),
        scratch_shapes=[
            held,
            pltpu.VMEM((steps, extent, rows, depth), jnp.float32),
            pltpu.SemaphoreType.DMA((2 * reach + 2,)),
        ],
        compiler_params=pltpu.CompilerParams(vmem_limit_bytes=60 * 1024 * 1024),
        cost_estimate=cost,
        name="adjoint",
    )(meta, *mine, *theirs, got, strains)
    end = lax.ppermute(end, axes, swap)
    parts = lax.all_to_all(grads, axes, 0, 0, axis_index_groups=pair, tiled=True)
    total = jnp.sum(parts, axis=0)
    return (end.reshape(1, 9, planes, rows, depth), total[0], total[1])


def solution(mesh):
    in_specs = (
        P("slab", None, None),
        P("slab", None, None),
        P("slab", None, None),
        P("shot", None, "slab", None, None),
        P("shot", None, "slab", None, None),
        P("shot", None),
        P("shot"),
        P("shot", None, "slab"),
        P("slab", None),
        P("slab"),
    )
    out_specs = (
        P("shot", None, "slab", None, None),
        P("slab", "shot", None),
        P("slab", "shot", None),
    )
    return jax.shard_map(shards, mesh=mesh, in_specs=in_specs, out_specs=out_specs, check_vma=False)
```

```python
import functools

import jax
import jax.numpy as jnp
from jax import lax
from jax.experimental import pallas as pl
from jax.experimental.pallas import tpu as pltpu
from jax.sharding import PartitionSpec as P

TIME_STEP = 0.3
CAP = 2
LANES = 128
FIELDS = 21
NOTES = 16


def reach_steps(steps, planes, reach):
    counts = {}
    for e in range(-reach, reach + 1):
        gap = planes * (abs(e) - 1) + 1 if e else 0
        counts[e] = max(0, steps - gap)
    return counts


def message_lanes(counts):
    lanes, at = {}, 0
    for e in sorted(counts, key=abs):
        for slot in range(CAP):
            lanes[e, slot] = at
            at += 1 + counts[e]
    return lanes, at


def split3(x):
    hi = x.astype(jnp.bfloat16)
    rest = x - hi.astype(jnp.float32)
    mid = rest.astype(jnp.bfloat16)
    low = (rest - mid.astype(jnp.float32)).astype(jnp.bfloat16)
    return hi, mid, low


def dot_onehot(values, onehot, dims):
    hi, mid, low = split3(values)
    hot = onehot.astype(jnp.bfloat16)
    go = lambda part: lax.dot_general(part, hot, dims, preferred_element_type=jnp.float32)
    return go(hi) + (go(mid) + go(low))


def onehot_dot(onehot, values, dims):
    hi, mid, low = split3(values)
    hot = onehot.astype(jnp.bfloat16)
    go = lambda part: lax.dot_general(hot, part, dims, preferred_element_type=jnp.float32)
    return go(hi) + (go(mid) + go(low))


def letters_kernel(counts, lanes, reach, steps, note_ref, out_ref, rows_ref):
    count = note_ref.shape[1]
    notes = note_ref[...]
    slab_row = jnp.broadcast_to(notes[steps : steps + 1], (count, count))
    slab_col = slab_row.T
    sub = lax.broadcasted_iota(jnp.int32, (count, count), 0)
    lane = lax.broadcasted_iota(jnp.int32, (count, count), 1)
    same = jnp.where((slab_col == slab_row) & (lane < sub), 1.0, 0.0)
    slot_of = jnp.sum(same, axis=1, keepdims=True)
    src = lax.broadcasted_iota(jnp.int32, (NOTES, LANES), 0)
    dst = lax.broadcasted_iota(jnp.int32, (NOTES, LANES), 1)
    spread = jnp.zeros((NOTES, LANES), jnp.float32)
    slot_lane = jnp.zeros((1, LANES), jnp.float32)
    one_lane = lax.broadcasted_iota(jnp.int32, (1, LANES), 1)
    for (e, slot), at in lanes.items():
        n = counts[e]
        spread = jnp.where((dst == at) & (src == steps + 1), 1.0, spread)
        spread = jnp.where((dst > at) & (dst <= at + n) & (src == dst - at - 1), 1.0, spread)
        slot_lane = jnp.where((one_lane >= at) & (one_lane <= at + n), float(slot), slot_lane)
    wide = dot_onehot(notes, spread, (((0,), (0,)), ((), ())))
    wide = jnp.where(slot_of == slot_lane, wide, 0.0)
    pick = jnp.where(slab_row == sub.astype(jnp.float32), 1.0, 0.0)
    rows = onehot_dot(pick, wide, (((1,), (0,)), ((), ())))
    rows_ref[...] = jnp.zeros_like(rows_ref)
    rows_ref[8 : 8 + count] = rows
    letter = jnp.zeros((count, LANES), jnp.float32)
    for e in range(-reach, reach + 1):
        start, end = lanes[e, 0], lanes[e, CAP - 1] + counts[e]
        letter = jnp.where((lane >= start) & (lane <= end), rows_ref[8 + e : 8 + e + count], letter)
    out_ref[...] = letter


def pack_kernel(cell_ref, f_ref, a_ref, lam_ref, mu_ref, buo_ref, trace_ref, slab_ref, spot_ref, wave_ref, out_ref):
    planes, rows, depth = lam_ref.shape
    one = planes * rows
    for c in range(9):
        out_ref[c * one : (c + 1) * one] = f_ref[c].reshape(one, depth)
        at = 12 * one + NOTES + c * one
        out_ref[at : at + one] = a_ref[c].reshape(one, depth)
    for c, ref in enumerate((lam_ref, mu_ref, buo_ref)):
        out_ref[(9 + c) * one : (10 + c) * one] = TIME_STEP * ref[...].reshape(one, depth)
    at, steps = 12 * one, trace_ref.shape[0]
    out_ref[at + 8 : at + NOTES] = jnp.zeros((NOTES - 8, depth), jnp.float32)
    out_ref[at : at + steps] = trace_ref[...]
    out_ref[at + steps : at + steps + 1] = slab_ref[...].astype(jnp.float32)
    out_ref[at + steps + 1 : at + steps + 2] = spot_ref[...].astype(jnp.float32)
    out_ref[at + steps + 2 : at + steps + 3, 0:steps] = wave_ref[...]
    out_ref[at + steps + 3 : at + steps + 4] = jnp.broadcast_to(cell_ref[...], (1, depth)).astype(jnp.float32)


class Window:
    def __init__(self, state, planes, rows, field, params, slab):
        self.state, self.planes, self.rows = state, planes, rows
        self.first = planes * slab
        self.one = planes * rows
        self.height = 12 * self.one + NOTES
        self.field, self.params = field, params
        self.own = pl.multiple_of(slab * self.height, 16)
        depth = state.shape[1]
        self.y = lax.broadcasted_iota(jnp.int32, (rows, depth), 0)
        self.z = lax.broadcasted_iota(jnp.int32, (rows, depth), 1)
        self.ends = (self.y == 0, self.y == rows - 1, self.z == 0, self.z == depth - 1)

    def fill(self, mine, theirs, sems, core, reach, start):
        copies = []
        for o in range(reach + 1):
            copies.append((mine[o], reach + core + (2 * core - 1) * o))
        for o in range(reach):
            copies.append((theirs[o], reach + 1 - core + (1 - 2 * core) * o))
        copies = [
            pltpu.make_async_copy(
                block.at[pl.ds(start, self.height)],
                self.state.at[pl.ds(pl.multiple_of(at * self.height, 16), self.height)],
                sems.at[i],
            )
            for i, (block, at) in enumerate(copies)
        ]
        for copy in copies:
            copy.start()
        return copies

    def base(self, p):
        return (p // self.planes) * self.height + (p % self.planes) * self.rows

    def at(self, base, row):
        return pl.ds(pl.multiple_of(self.own + (base + row), 8), self.rows)

    def get(self, base, c):
        return self.state[self.at(base, self.field + c * self.one)]

    def param(self, base, c):
        return self.state[self.at(base, self.params + c * self.one)]

    def put(self, base, values):
        for c, value in values:
            self.state[self.at(base, self.field + c * self.one)] = value

    def prev_y(self, x):
        return jnp.where(self.ends[0], 0.0, pltpu.roll(x, 1, 0))

    def next_y(self, x):
        return jnp.where(self.ends[1], 0.0, pltpu.roll(x, x.shape[0] - 1, 0))

    def prev_z(self, x):
        return jnp.where(self.ends[2], 0.0, pltpu.roll(x, 1, 1))

    def next_z(self, x):
        return jnp.where(self.ends[3], 0.0, pltpu.roll(x, x.shape[1] - 1, 1))

    def velocity(self, p, along_x=True, across=True):
        here, after, before = self.base(p), self.base(p + 1), self.base(p - 1)
        get = self.get
        factor = self.param(here, 2)
        sxy, sxz = get(here, 6), get(here, 7)
        out = []
        if along_x:
            accel = (get(after, 3) - get(here, 3)) + (sxy - self.prev_y(sxy)) + (sxz - self.prev_z(sxz))
            out.append((0, get(here, 0) - factor * accel))
        if across:
            syy, szz, syz = get(here, 4), get(here, 5), get(here, 8)
            accel = (sxy - get(before, 6)) + (self.next_y(syy) - syy) + (syz - self.prev_z(syz))
            out.append((1, get(here, 1) - factor * accel))
            accel = (sxz - get(before, 7)) + (syz - self.prev_y(syz)) + (self.next_z(szz) - szz)
            out.append((2, get(here, 2) - factor * accel))
        return here, out

    def stress(self, p, push=None):
        here, after, before = self.base(p), self.base(p + 1), self.base(p - 1)
        get = self.get
        lam, mu = self.param(here, 0), self.param(here, 1)
        twice = 2.0 * mu
        vx, vy, vz = get(here, 0), get(here, 1), get(here, 2)
        exx = vx - get(before, 0)
        eyy = vy - self.prev_y(vy)
        ezz = vz - self.prev_z(vz)
        exy = (self.next_y(vx) - vx) + (get(after, 1) - vy)
        exz = (self.next_z(vx) - vx) + (get(after, 2) - vz)
        eyz = (self.next_z(vy) - vy) + (self.next_y(vz) - vz)
        volume = lam * (exx + eyy + ezz)
        if push is not None:
            volume = volume + push
        out = [
            (3, get(here, 3) - (volume + twice * exx)),
            (4, get(here, 4) - (volume + twice * eyy)),
            (5, get(here, 5) - (volume + twice * ezz)),
            (6, get(here, 6) - mu * exy),
            (7, get(here, 7) - mu * exz),
            (8, get(here, 8) - mu * eyz),
        ]
        return here, out, (exx, eyy, ezz, exy, exz, eyz)

    def step(self, k, steps, push, see):
        m = steps - 1 - k
        low, high = -m, self.planes + m
        pushed = lambda p: None if push is None else push[k, self.first + p]
        ready = []
        for p in range(low - 1, high + 1):
            ready.append(self.velocity(p, along_x=p < high, across=p >= low))
            if p >= low:
                self.put(*ready.pop(0))
        self.put(*ready.pop(0))
        for p in range(low, high):
            here, out, strains = self.stress(p, pushed(p))
            self.put(here, out)
            if 0 <= p < self.planes:
                see(k, p, strains)


def forward_kernel(reach, steps, planes, rows, meta_ref, *refs):
    mine, theirs = refs[: reach + 1], refs[reach + 1 : 2 * reach + 1]
    strain_ref, state, sems = refs[2 * reach + 1 :]
    depth = state.shape[1]
    one = planes * rows
    core, slab = meta_ref[0], meta_ref[1]
    window = Window(state, planes, rows, 0, 9 * one, reach + core)
    for copy in window.fill(mine, theirs, sems, core, reach, 0):
        copy.wait()
    halo = planes * (reach + core)
    at = pl.multiple_of((reach + core) * window.height + 12 * one + steps, 8)
    notes = state[pl.ds(at, 8)]
    wave, cell = notes[2:3], jnp.max(notes[3:4]).astype(jnp.int32)
    src_plane = cell // (rows * depth) - planes * slab
    spot = jnp.where(window.y * depth + window.z == cell % (rows * depth), TIME_STEP, 0.0)

    def see(k, p, strains):
        for c, strain in enumerate(strains):
            strain_ref[k, c, p] = strain

    for k in range(steps):
        window.step(k, steps, None, see)
        m = steps - 1 - k

        @pl.when((src_plane >= -m) & (src_plane < planes + m))
        def _():
            shot = wave[:, k : k + 1] * spot
            there = window.base(src_plane + planes * reach) - reach * window.height
            window.put(there, [(c, window.get(there, c) - shot) for c in (3, 4, 5)])


def adjoint_kernel(counts, lanes, reach, steps, planes, rows, meta_ref, *refs):
    mine, theirs = refs[: reach + 1], refs[reach + 1 : 2 * reach + 1]
    letters_ref, strain_ref, end_ref, grad_ref, state, push, sems = refs[2 * reach + 1 :]
    depth = state.shape[1]
    one = planes * rows
    core = meta_ref[0]
    window = Window(state, planes, rows, 3 * one + NOTES, 0, reach + core)
    copies = window.fill(mine, theirs, sems, core, reach, 9 * one)
    halo = planes * (reach + core)
    letters = letters_ref[...]
    letters_t = letters.T
    sources = letters.shape[0]
    lane_iota = lax.broadcasted_iota(jnp.int32, (sources, depth), 1)
    row_iota = lax.broadcasted_iota(jnp.int32, (one, sources), 0)
    for e in range(-reach, reach + 1):
        n = counts[e]
        lefts, rights = [], []
        for slot in range(CAP):
            at = lanes[e, slot]
            cell_col = letters[:, at : at + 1].astype(jnp.int32)
            rights.append(jnp.where(lane_iota == (cell_col & (depth - 1)), 1.0, 0.0))
            cell_row = letters_t[at : at + 1, :].astype(jnp.int32) // depth
            hit = row_iota == cell_row
            lefts.append(
                jnp.concatenate([jnp.where(hit, letters_t[at + 1 + k : at + 2 + k, :], 0.0) for k in range(n)], axis=0)
            )
        left = jnp.concatenate(lefts, axis=1)
        right = jnp.concatenate(rights, axis=0)
        sums = TIME_STEP * dot_onehot(left, right, (((1,), (0,)), ((), ())))
        for k in range(n):
            push[k, pl.ds(halo + planes * e, planes)] = sums[k * one : (k + 1) * one].reshape(planes, rows, depth)
    for copy in copies:
        copy.wait()

    totals = [[jnp.zeros((rows, depth), jnp.float32)] * 2 for _ in range(planes)]

    def see(k, p, strains):
        axx, ayy, azz, axy, axz, ayz = (strain_ref[k, c, p] for c in range(6))
        bxx, byy, bzz, bxy, bxz, byz = strains
        first = (axx + ayy + azz) * (bxx + byy + bzz)
        second = 2.0 * (axx * bxx + ayy * byy + azz * bzz) + axy * bxy + axz * bxz + ayz * byz
        totals[p] = [totals[p][0] + first, totals[p][1] + second]

    for k in range(steps):
        window.step(k, steps, push, see)

    own = pl.multiple_of((reach + core) * window.height + window.field, 16)
    final = pltpu.make_async_copy(state.at[pl.ds(own, 9 * one)], end_ref, sems.at[2 * reach + 1])
    final.start()
    shots = grad_ref.shape[0] // 2
    share = rows // shots
    for p in range(planes):
        for g in range(2):
            total = TIME_STEP * totals[p][g]
            for j in range(shots):
                for h in range(2):
                    grad_ref[2 * j + h, g, p] = jnp.where(core == h, total[j * share : (j + 1) * share], 0.0)
    final.wait()


def vmem():
    return pl.BlockSpec(memory_space=pltpu.VMEM)


def smem():
    return pl.BlockSpec(memory_space=pltpu.SMEM)


def hbm():
    return pl.BlockSpec(memory_space=pltpu.HBM)


def shards(
    lame_lambda,
    lame_mu,
    buoyancy,
    forward_state,
    adjoint_state,
    source_wavelet,
    source_cell,
    residual_traces,
    receiver_slab,
    receiver_cell,
):
    planes, rows, depth = lame_lambda.shape
    one = planes * rows
    steps = source_wavelet.shape[1]
    slabs = lax.axis_size("slab")
    shots = lax.axis_size("shot")
    axes = ("shot", "slab")
    reach = -(-steps // planes)
    counts = reach_steps(steps, planes, reach)
    lanes, _ = message_lanes(counts)
    height = FIELDS * one + NOTES

    def at(s, d):
        return ((s & ~1) | (d & 1)) * slabs + ((d & ~1) | (s & 1))

    every = [(s, d) for s in range(shots) for d in range(slabs)]
    swap = [(s * slabs + d, at(s, d)) for s, d in every]
    across = [(at(s, d), at(s, d ^ 1)) for s, d in every]
    team = [[at(s, d) for d in range(slabs)] for s in range(shots)]
    pair = [[s * slabs + 2 * q + h for s in range(shots) for h in range(2)] for q in range(slabs // 2)]

    block = pl.pallas_call(
        pack_kernel,
        out_shape=jax.ShapeDtypeStruct((height, depth), jnp.float32),
        in_specs=[vmem()] * 10,
        out_specs=vmem(),
        name="pack",
    )(
        source_cell.reshape(1, 1),
        forward_state[0],
        adjoint_state[0],
        lame_lambda,
        lame_mu,
        buoyancy,
        residual_traces[0],
        receiver_slab.reshape(1, -1),
        receiver_cell.reshape(1, -1),
        source_wavelet,
    )
    mine = [lax.ppermute(block, axes, swap)]
    for o in range(1, reach + 1):
        pairs = []
        for s, d in every:
            i = d + o if d % 2 else d - o
            if 0 <= i < slabs:
                pairs.append((s * slabs + i, at(s, d)))
        mine.append(lax.ppermute(block, axes, pairs))

    letters = pl.pallas_call(
        functools.partial(letters_kernel, counts, lanes, reach, steps),
        grid=(1,),
        out_shape=jax.ShapeDtypeStruct((slabs, LANES), jnp.float32),
        in_specs=[pl.BlockSpec((NOTES, depth), lambda i: (12 * one // NOTES, 0))],
        out_specs=pl.BlockSpec((slabs, LANES), lambda i: (0, 0)),
        scratch_shapes=[pltpu.VMEM((slabs + 16, LANES), jnp.float32)],
        name="letters",
    )(mine[0])
    got = lax.all_to_all(letters, axes, 0, 0, axis_index_groups=team, tiled=True)
    my_shot, my_slab = lax.axis_index("shot"), lax.axis_index("slab")
    core = my_shot & 1
    meta = jnp.stack([core, (my_slab & ~1) | core]).astype(jnp.int32)
    extent = planes * (2 * reach + 2)
    held = pltpu.VMEM(((2 * reach + 2) * (12 * one + NOTES), depth), jnp.float32)
    cost = pl.CostEstimate(flops=60_000_000, transcendentals=0, bytes_accessed=16_000_000)

    def share(blocks):
        return [lax.ppermute(block, axes, across) for block in blocks]

    here = my_slab < slabs
    theirs = []
    theirs += lax.cond(here, share, lambda blocks: blocks, mine[0:2])
    theirs += lax.cond(here, share, lambda blocks: blocks, mine[2:3])
    theirs += lax.cond(here, share, lambda blocks: blocks, mine[3:reach])

    def run(blocks):
        strains = pl.pallas_call(
            functools.partial(forward_kernel, reach, steps, planes, rows),
            out_shape=jax.ShapeDtypeStruct((steps, 6, planes, rows, depth), jnp.float32),
            in_specs=[smem()] + [hbm()] * (2 * reach + 1),
            out_specs=vmem(),
            scratch_shapes=[held, pltpu.SemaphoreType.DMA((2 * reach + 1,))],
            compiler_params=pltpu.CompilerParams(vmem_limit_bytes=60 * 1024 * 1024),
            cost_estimate=cost,
            name="forward",
        )(meta, *blocks)
        return strains

    strains = lax.cond(here, run, lambda blocks: jnp.zeros((steps, 6, planes, rows, depth), jnp.float32), (*mine, *theirs))
    end, grads = pl.pallas_call(
        functools.partial(adjoint_kernel, counts, lanes, reach, steps, planes, rows),
        out_shape=(
            jax.ShapeDtypeStruct((9 * one, depth), jnp.float32),
            jax.ShapeDtypeStruct((2 * shots, 2, planes, rows // shots, depth), jnp.float32),
        ),
        in_specs=[smem()] + [hbm()] * (2 * reach + 1) + [vmem()] * 2,
        out_specs=(hbm(), vmem()),
        scratch_shapes=[
            held,
            pltpu.VMEM((steps, extent, rows, depth), jnp.float32),
            pltpu.SemaphoreType.DMA((2 * reach + 2,)),
        ],
        compiler_params=pltpu.CompilerParams(vmem_limit_bytes=60 * 1024 * 1024),
        cost_estimate=cost,
        name="adjoint",
    )(meta, *mine, *theirs, got, strains)
    end = lax.ppermute(end, axes, swap)
    parts = lax.all_to_all(grads, axes, 0, 0, axis_index_groups=pair, tiled=True)
    total = jnp.sum(parts, axis=0)
    return (end.reshape(1, 9, planes, rows, depth), total[0], total[1])


def solution(mesh):
    in_specs = (
        P("slab", None, None),
        P("slab", None, None),
        P("slab", None, None),
        P("shot", None, "slab", None, None),
        P("shot", None, "slab", None, None),
        P("shot", None),
        P("shot"),
        P("shot", None, "slab"),
        P("slab", None),
        P("slab"),
    )
    out_specs = (
        P("shot", None, "slab", None, None),
        P("slab", "shot", None),
        P("slab", "shot", None),
    )
    return jax.shard_map(shards, mesh=mesh, in_specs=in_specs, out_specs=out_specs, check_vma=False)
```
